256 devices in a mesh: gx: 4 (over x), gy: 16 (over z, core), gz: 4 (over y).
Axes of the slice: x: 4, y: 4, z: 8, core: 2. Of those that a mesh axis runs over, the one named last changes fastest.
Arguments:
- right_side: float32 [8, 64, 256, 512], P(None, 'gx', 'gy', 'gz'), may hold values from -12 to 12
- potential: float32 [64, 256, 512], P('gx', 'gy', 'gz'), may hold values from 0.2 to 2
- orbital_shift: float32 [8], replicated, may hold values from 0.2 to 1
- projector: float32 [4096, 4, 32, 128], P(('gx', 'gy', 'gz')), may hold values from -0.5 to 0.5
- coupling: float32 [4096, 4], P(('gx', 'gy', 'gz')), may hold values from 0.25 to 2
- block_ids: int32 [4096, 32], P(('gx', 'gy', 'gz')), may hold values from 0 to 1023, all different within a row
Outputs:
- solution: float32 [8, 64, 256, 512], P(None, 'gx', 'gy', 'gz')
- residual: float32 [8, 64, 256, 512], P(None, 'gx', 'gy', 'gz')
The draws below stay inside these ranges and needn't reach their ends.
Inputs may be any that keep to these rules, and one draw needn't show every extreme that they name: `block_ids`: each row names 32 different blocks of the column of domains of the atom's owner, numbered as in the reference program.
All inputs are finite; a program needn't handle non-finite values.
Results may differ from the reference program's by a relative error of at most 0.00022.
Values sent between devices are 32-bit elements; how exact they have to be, the bound alone decides.
No kernel may reach another device: no remote copies, remote signals or barrier semaphores. Data moves between devices by JAX's collectives and lax.ppermute only.
A program may use at most 128 MiB of HBM per device.

```python
import math
import jax
import jax.numpy as jnp
from jax import lax

CX = 16
CY = 16
CZ = 128
ATOM_DEV = 16
ORB = 8
PROJ = 4
NB = 32
ITERS = 2
NX = 64
NY = 256
NZ = 512
ATOMS = 4096
N_GY = 16
N_GZ = 4


def draw_right_side(key, part):
    pos_x = jnp.arange(NX, dtype=jnp.float32) / NX
    pos_y = jnp.arange(NY, dtype=jnp.float32) / NY
    pos_z = jnp.arange(NZ, dtype=jnp.float32) / NZ
    slope = (pos_x[:, None, None] + pos_y[None, :, None] + pos_z[None, None, :]) / 3.0
    base = jnp.clip(jax.random.normal(key, (ORB, NX, NY, NZ), jnp.float32), -4.0, 4.0)
    return base * (1.0 + 2.0 * slope)[None]


def steps_of(stream_key, extent, pieces, smallest, largest):
    def one(dim, blocks):
        heights = jax.random.uniform(jax.random.fold_in(jax.random.fold_in(stream_key, 6), dim), (blocks,), jnp.float32, smallest / len(pieces), largest / len(pieces))
        return jnp.repeat(jnp.exp(heights), extent[dim] // blocks).reshape((-1,) + (1,) * (len(extent) - dim - 1))

    gain = one(*pieces[0])
    for cut in pieces[1:]:
        gain = gain * one(*cut)
    return gain


def picks_of(key, rows, count, top, lift):
    order = jax.random.permutation(jax.random.fold_in(key, 1), count)
    favour = order
    for power in range(3):
        favour = favour * favour // count
    favour = favour * lift // count
    chance = jax.random.randint(jax.random.fold_in(key, 2), (rows, count), 0, 4096) + favour
    sure = jax.random.permutation(jax.random.fold_in(key, 3), rows)[jnp.arange(count) % rows]
    chance = jnp.where(jnp.arange(rows)[:, None] == sure[None, :], 1 << 14, chance)
    merit = chance * count + jnp.arange(count)
    return lax.top_k(merit.astype(jnp.int32), top)[1].astype(jnp.int32)


def gaussian(rng, shape, deviation, most, split=(), held_as=jnp.bfloat16):
    loudness = steps_of(rng, shape, split, -0.22, 0.18) if split else 1.0
    drawn = jax.random.normal(rng, shape, jnp.float32) * deviation * loudness
    return jnp.minimum(jnp.maximum(drawn, -most), most).astype(held_as)


def setup_inputs(seed: int = 0) -> dict:
    key_of = jax.random.split(jax.random.key(seed), 7)
    right_side = draw_right_side(jax.random.fold_in(key_of[6], 71), 0)
    potential = jnp.clip(0.2 + 1.8 * jax.random.uniform(key_of[1], (NX, NY, NZ), jnp.float32) ** steps_of(key_of[1], (NX, NY, NZ), ((0, 4), (1, 16), (2, 4)), -0.2, 0.2), 0.2, 2.0)
    orbital_shift = jnp.clip(jax.random.uniform(key_of[2], (ORB,), jnp.float32, 0.2, 1.0), 0.2, 1.0)
    projector = gaussian(key_of[3], (ATOMS, PROJ, NB, CZ), 0.08, 0.5, ((0, 256),), jnp.float32)
    coupling = jnp.clip(jnp.exp(math.log(2.0) - 2.0794415 * jax.random.uniform(key_of[4], (ATOMS, PROJ), jnp.float32) ** steps_of(key_of[4], (ATOMS, PROJ), ((0, 256),), -0.2, 0.2)), 0.25, 2.0)
    block_ids = picks_of(key_of[5], ATOMS, N_GZ * CX * CY, NB, 256)
    return dict(right_side=right_side, potential=potential, orbital_shift=orbital_shift, projector=projector, coupling=coupling, block_ids=block_ids)


STENCIL = (-5369.0 / 1800.0, 12.0 / 7.0, -15.0 / 56.0, 10.0 / 189.0, -1.0 / 112.0, 2.0 / 1925.0, -1.0 / 16632.0)


def laplace(padded, size_x, size_y, size_z):
    summed = 3.0 * STENCIL[0] * padded[..., 6:6 + size_x, 6:6 + size_y, 6:6 + size_z]
    for reach in range(1, 7):
        summed = summed + STENCIL[reach] * (
            padded[..., 6 + reach:6 + reach + size_x, 6:6 + size_y, 6:6 + size_z]
            + padded[..., 6 - reach:6 - reach + size_x, 6:6 + size_y, 6:6 + size_z]
            + padded[..., 6:6 + size_x, 6 + reach:6 + reach + size_y, 6:6 + size_z]
            + padded[..., 6:6 + size_x, 6 - reach:6 - reach + size_y, 6:6 + size_z]
            + padded[..., 6:6 + size_x, 6:6 + size_y, 6 + reach:6 + reach + size_z]
            + padded[..., 6:6 + size_x, 6:6 + size_y, 6 - reach:6 - reach + size_z])
    return summed


def column_index(block_ids):
    atom_row = jnp.arange(ATOMS, dtype=jnp.int32)
    owner = atom_row // ATOM_DEV
    owner_x = owner // (N_GY * N_GZ)
    owner_y = (owner // N_GZ) % N_GY
    source = block_ids // (CX * CY)
    within = block_ids % (CX * CY)
    cell_x = owner_x[:, None] * CX + within // CY
    cell_y = owner_y[:, None] * CY + within % CY
    return ((cell_x * NY + cell_y) * N_GZ + source).astype(jnp.int32)


def nonlocal_term(fields, projector, coupling, lines):
    flat_lines = lines.reshape(-1)

    def single(values):
        columns = values.reshape(NX * NY * N_GZ, CZ)
        picked = columns[flat_lines].reshape(ATOMS, NB, CZ)
        projected = jnp.einsum('akz,apkz->ap', picked, projector, precision=lax.Precision.HIGHEST)
        weights = projected * coupling
        contribution = jnp.einsum('ap,apkz->akz', weights, projector, precision=lax.Precision.HIGHEST)
        placed = jnp.zeros((NX * NY * N_GZ, CZ), jnp.float32).at[flat_lines].add(contribution.reshape(-1, CZ))
        return placed.reshape(NX, NY, NZ)

    return lax.map(single, fields)


def reference(right_side, potential, orbital_shift, projector, coupling, block_ids):
    lines = column_index(block_ids)
    diagonal = potential[None] + orbital_shift[:, None, None, None]

    def operate(fields):
        padded = jnp.pad(fields, ((0, 0), (6, 6), (6, 6), (6, 6)))
        return -0.5 * laplace(padded, NX, NY, NZ) + diagonal * fields + nonlocal_term(fields, projector, coupling, lines)

    solution = jnp.zeros_like(right_side)
    residual = right_side
    direction = right_side
    norm_now = jnp.sum(residual * residual, axis=(1, 2, 3))
    for sweep in range(ITERS):
        image = operate(direction)
        step_len = norm_now / jnp.sum(direction * image, axis=(1, 2, 3))
        solution = solution + step_len[:, None, None, None] * direction
        residual = residual - step_len[:, None, None, None] * image
        norm_next = jnp.sum(residual * residual, axis=(1, 2, 3))
        direction = residual + (norm_next / norm_now)[:, None, None, None] * direction
        norm_now = norm_next
    return solution, residual
```

```python
import functools

import jax
import jax.numpy as jnp
import numpy as np
from jax import lax
from jax.experimental import pallas as pl
from jax.experimental.pallas import tpu as pltpu
from jax.sharding import PartitionSpec as P


STENCIL = (
    -5369.0 / 1800.0,
    12.0 / 7.0,
    -15.0 / 56.0,
    10.0 / 189.0,
    -1.0 / 112.0,
    2.0 / 1925.0,
    -1.0 / 16632.0,
)
GRID = ("gx", "gy", "gz")
F32 = jnp.float32
BF16 = jnp.bfloat16
VM = pl.BlockSpec(memory_space=pltpu.VMEM)
SM = pl.BlockSpec(memory_space=pltpu.SMEM)
NN = (((1,), (0,)), ((), ()))
NT = (((1,), (1,)), ((), ()))
TN = (((0,), (0,)), ((), ()))

PIECES = (16, 16, 16, 8, 8)
OFFSETS = (0, -1, 1, 2)


def slot_of(offset):
    return {0: 0, 3: 1, 1: 2, 2: 3}[offset % 4]


def weight(step):
    step = abs(step)
    return -0.5 * STENCIL[step] if 0 < step <= 6 else 0.0


def plane_matrix():
    mat = np.zeros((256, 704))
    for x in range(16):
        for y in range(16):
            row = x * 16 + y
            mat[row, row] = -0.5 * 3.0 * STENCIL[0]
            for reach in range(1, 7):
                for step in (reach, -reach):
                    to_x, to_y = x + step, y + step
                    if 0 <= to_x < 16:
                        mat[row, to_x * 16 + y] += weight(reach)
                    elif to_x < 0:
                        mat[row, 256 + (to_x + 6) * 16 + y] += weight(reach)
                    else:
                        mat[row, 352 + (to_x - 16) * 16 + y] += weight(reach)
                    if 0 <= to_y < 16:
                        mat[row, x * 16 + to_y] += weight(reach)
                    elif to_y < 0:
                        mat[row, 448 + x * 8 + (to_y + 8)] += weight(reach)
                    else:
                        mat[row, 576 + x * 8 + (to_y - 16)] += weight(reach)
    return mat


def z_matrix():
    mat = np.zeros((128, 128))
    for z in range(128):
        for step in range(-6, 7):
            if 0 <= z + step < 128:
                mat[z + step, z] += weight(step)
    return mat


def z_halo_matrix():
    mat = np.zeros((16, 128))
    for z in range(128):
        for reach in range(1, 7):
            if z - reach < 0:
                mat[z - reach + 6, z] += weight(reach)
            if z + reach >= 128:
                mat[8 + z + reach - 128, z] += weight(reach)
    return mat


def pick_matrix():
    mat = np.zeros((16, 128))
    for cell in range(6):
        mat[cell, 122 + cell] = 1.0
        mat[8 + cell, cell] = 1.0
    return mat


def two_parts(mat):
    high = mat.astype(np.float32).astype(BF16)
    low = (mat - high.astype(np.float64)).astype(np.float32).astype(BF16)
    return high, low


def constants():
    plane = two_parts(plane_matrix())
    z_band = np.concatenate(two_parts(z_matrix()))
    z_halo = np.concatenate(two_parts(z_halo_matrix()))
    pick = pick_matrix().astype(np.float32).astype(BF16)
    ones = np.ones((16, 128), np.float32).astype(BF16)
    return tuple(jnp.asarray(part) for part in (*plane, z_band, z_halo, pick, ones))


def dot(lhs, rhs, dims):
    return lax.dot_general(lhs, rhs, dims, preferred_element_type=F32)


def split2(value):
    high = value.astype(BF16)
    return high, (value - high.astype(F32)).astype(BF16)


def split3(value):
    high = value.astype(BF16)
    rest = value - high.astype(F32)
    mid = rest.astype(BF16)
    return high, mid, (rest - mid.astype(F32)).astype(BF16)


def iota(shape, dim):
    return lax.broadcasted_iota(jnp.int32, shape, dim)


def store_z_faces(value, pick, up_ref, down_ref):
    high, mid, low = split3(value)
    faces = dot(pick, high, NT) + dot(pick, mid, NT) + dot(pick, low, NT)
    up_ref[...] = faces[:8]
    down_ref[...] = faces[8:]


def z_faces_kernel(v_ref, pick_ref, up_ref, down_ref):
    store_z_faces(v_ref[...], pick_ref[...], up_ref, down_ref)


def stencil_kernel(last, shift_ref, v_ref, xl, xh, yl, yh, zl, zh, pot, kh_ref, kl_ref, zb_ref, zc_ref, *rest):
    if last:
        add_ref, moment_ref, out_ref, sent_ref = rest
    else:
        (out_ref,) = rest
    plane_high, plane_low = kh_ref[...], kl_ref[...]
    edge_high, edge_low = split2(jnp.concatenate([zl[...], zh[...]], axis=0))
    z_halo, z_band = zc_ref[...], zb_ref[...]
    lane, row = iota((8, 128), 1), iota((8, 128), 0)
    moment = jnp.zeros((8, 128), F32)
    for first in range(0, 8, 2):
        pair = (first, first + 1)
        columns = [jnp.concatenate([v_ref[n], xl[n], xh[n], yl[n], yh[n]], axis=0) for n in pair]
        high, low = split2(jnp.concatenate(columns, axis=1))
        plane = dot(plane_high, high, NN) + dot(plane_high, low, NN) + dot(plane_low, high, NN)
        for i, n in enumerate(pair):
            lanes = slice(i * 128, (i + 1) * 128)
            own_high, own_low = high[:256, lanes], low[:256, lanes]
            out = plane[:, lanes] + dot(own_high, z_band[:128], NN)
            out = out + dot(own_low, z_band[:128], NN) + dot(own_high, z_band[128:], NN)
            above, below = edge_high[:, n * 256 : (n + 1) * 256], edge_low[:, n * 256 : (n + 1) * 256]
            out = out + dot(above, z_halo[:16], TN) + dot(below, z_halo[:16], TN) + dot(above, z_halo[16:], TN)
            value = v_ref[n]
            out = out + (pot[...] + shift_ref[n]) * value
            if last:
                out = out + add_ref[n]
                moment = jnp.where((lane == 3) & (row == n), jnp.sum(value * out), moment)
            out_ref[n] = out
    if last:
        moment = moment + moment_ref[...]
        flat = jnp.zeros((8, 128), F32)
        for i in range(4):
            flat = flat + jnp.where(lane == i * 8 + row, moment[:, i : i + 1], 0.0)
        sent_ref[...] = jnp.broadcast_to(jnp.sum(flat, axis=0, keepdims=True), sent_ref.shape)


def to_lines(src, dst):
    def eight(i, carry):
        for u in range(8):
            line = i * 8 + u
            dst[line] = src[pl.ds(line, 8, stride=256), :]
        return carry

    lax.fori_loop(0, 32, eight, 0)


def project_kernel(counts, start, ids_ref, v_ref, *rest):
    pieces, rest = rest[: len(counts)], rest[len(counts) :]
    ones_ref, *before, out_ref, lines, sums_ref = rest
    to_lines(v_ref, lines)
    lines[256] = jnp.zeros((8, 128), F32)
    base = start
    for ref, count in zip(pieces, counts):

        def atom(a, carry, ref=ref, base=base):
            sums = [jnp.zeros((8, 128), F32) for _ in range(4)]
            for k in range(32):
                value = lines[ids_ref[(base + a) * 32 + k]]
                for j in range(4):
                    sums[j] = sums[j] + value * ref[pl.ds((a * 4 + j) * 32 + k, 8, stride=0), :]
            for j in range(4):
                sums_ref[pl.ds(pl.multiple_of(((base - start + a) * 4 + j) * 8, 8), 8), :] = sums[j]
            return carry

        lax.fori_loop(0, count, atom, 0)
        base += count
    high, mid, low = split3(sums_ref[...])
    ones = ones_ref[...]
    total = dot(ones, high, NT) + dot(ones, mid, NT) + dot(ones, low, NT)
    if before:
        out_ref[...] = before[0][...]
    for r in range(start // 16, base // 16):
        at = r * 512 - start * 32
        out_ref[r : r + 1, :] = total[0:1, at : at + 512]


def place_kernel(first, ids_ref, here, lower, upper, opposite, coupling_ref, *rest):
    pieces, ones_ref = rest[:5], rest[5]
    if first:
        base_ref, b_ref, pick_ref = rest[6:9]
        out_ref, x_up, x_down, y_up, y_down, z_up, z_down, moment_ref, weights, lines = rest[9:]
    else:
        out_ref, weights, lines = rest[6:]
    rows = []
    for r in range(4):
        total = here[r : r + 1, :]
        for ref, away in ((lower, -1), (upper, 1), (opposite, 2)):
            slot = slot_of(OFFSETS[r] - away)
            total = total + ref[slot : slot + 1, :]
        rows.append(total * coupling_ref[r : r + 1, :])
    high, mid, low = (part.astype(F32) for part in split3(jnp.concatenate(rows, axis=1)))
    row = iota((16, 2048), 0)
    stacked = jnp.where(row == 0, high, jnp.where(row == 1, mid, jnp.where(row == 2, low, 0.0)))
    weights[...] = dot(stacked.astype(BF16), ones_ref[...], TN)
    if first:
        to_lines(base_ref, lines)
    else:
        lines[...] = jnp.zeros_like(lines)
    base = 0
    for ref, count in zip(pieces, PIECES):

        def atom(a, carry, ref=ref, base=base):
            of = [weights[pl.ds(pl.multiple_of(((base + a) * 4 + j) * 8, 8), 8), :] for j in range(4)]
            for chunk in range(4):
                at = [ids_ref[(base + a) * 32 + chunk * 8 + k] for k in range(8)]
                values = [lines[line] for line in at]
                for k in range(8):
                    terms = [
                        of[j] * ref[pl.ds((a * 4 + j) * 32 + chunk * 8 + k, 8, stride=0), :] for j in range(4)
                    ]
                    values[k] = values[k] + ((terms[0] + terms[1]) + (terms[2] + terms[3]))
                for k in range(8):
                    lines[at[k]] = values[k]
            return carry

        lax.fori_loop(0, count, atom, 0)
        base += count
    if not first:

        def back(i, carry):
            for u in range(8):
                line = i * 8 + u
                out_ref[pl.ds(line, 8, stride=256), :] = lines[line]
            return carry

        lax.fori_loop(0, 32, back, 0)
        return

    def finish(i, moments):
        m0, m1, m2 = moments
        for u in range(8):
            line = i * 8 + u
            image, value = lines[line], b_ref[pl.ds(line, 8, stride=256), :]
            out_ref[pl.ds(line, 8, stride=256), :] = image
            m0, m1, m2 = m0 + value * value, m1 + value * image, m2 + image * image
        return m0, m1, m2

    zero = jnp.zeros((8, 128), F32)
    moments = lax.fori_loop(0, 32, finish, (zero, zero, zero))
    lane = iota((8, 128), 1)
    stored = zero
    for i in range(3):
        stored = jnp.where(lane == i, jnp.sum(moments[i], axis=1, keepdims=True), stored)
    moment_ref[...] = stored
    image = out_ref[...]
    store_z_faces(image, pick_ref[...], z_up, z_down)
    by_x = image.reshape(8, 256, 128)
    x_up[...] = by_x[:, 160:]
    x_down[...] = by_x[:, :96]
    by_y = image.reshape(128, 2, 8, 128)
    y_up[...] = by_y[:, 1].reshape(8, 128, 128)
    y_down[...] = by_y[:, 0].reshape(8, 128, 128)


def finish_kernel(moments_ref, b_ref, w1_ref, w2_ref, solution_ref, residual_ref):
    flat = jnp.sum(moments_ref[...], axis=0, keepdims=True)
    m0, m1, m2, m3 = (flat[:, i * 8 : (i + 1) * 8] for i in range(4))
    alpha = m0 / m1
    fresh = alpha * (alpha * m2 - 2.0 * m1) + m0
    product = m1 + alpha * (alpha * m3 - 2.0 * m2)
    beta = fresh / m0
    alpha2 = fresh / (product - beta * fresh / alpha)
    s1 = alpha + alpha2 * (1.0 + beta)
    s2 = alpha * alpha2
    for n in range(8):
        one, two = s1[:, n : n + 1], s2[:, n : n + 1]
        b, w1, w2 = b_ref[n], w1_ref[n], w2_ref[n]
        solution_ref[n] = one * b - two * w1
        residual_ref[n] = b - one * w1 + two * w2


def shape(*dims):
    return jax.ShapeDtypeStruct(dims, F32)


def call(kernel, name, args, outs, scratch=(), scalars=1, flops=0, moved=1 << 20):
    many = isinstance(outs, tuple)
    return pl.pallas_call(
        kernel,
        out_shape=outs,
        in_specs=[SM] * scalars + [VM] * (len(args) - scalars),
        out_specs=(VM,) * len(outs) if many else VM,
        scratch_shapes=scratch,
        name=name,
        cost_estimate=pl.CostEstimate(flops=flops, bytes_accessed=moved, transcendentals=0),
    )(*args)


LINE_SCRATCH = pltpu.VMEM((264, 8, 128), F32)
ATOM_SCRATCH = pltpu.VMEM((2048, 128), F32)


def on_device(right_side, potential, orbital_shift, projector, coupling, block_ids):
    plane_high, plane_low, z_band, z_halo, pick, ones = constants()
    bands = (plane_high, plane_low, z_band, z_halo)
    b = right_side.reshape(8, 256, 128)
    pot = potential.reshape(256, 128)
    own = projector.reshape(2048, 128)
    around = {shift: [(i, (i + shift) % 4) for i in range(4)] for shift in (1, -1, 2)}

    def beside(array):
        return tuple(lax.ppermute(array, "gz", around[shift]) for shift in (1, -1, 2))

    lower = lax.ppermute(own, "gz", around[1])
    upper = lax.ppermute(own, "gz", around[-1])
    pieces = (
        own,
        lower,
        upper,
        lax.ppermute(lower[:1024], "gz", around[1]),
        lax.ppermute(upper[1024:], "gz", around[-1]),
    )
    side = jnp.concatenate(
        [block_ids.astype(F32).reshape(512), coupling.reshape(64), jnp.zeros((448,), F32)]
    ).reshape(8, 128)
    sides = jnp.stack((side, *beside(side)))
    ids = sides[:, :4].reshape(2048).astype(jnp.int32) - 256 * lax.axis_index("gz")
    ids = jnp.where((ids >= 0) & (ids < 256), ids, 256)
    couplings = jnp.repeat(sides[:, 4, :64], 8, axis=1)

    def line(axis, step):
        size = lax.axis_size(axis)
        return [(i, i + step) for i in range(size) if 0 <= i + step < size]

    def halos(x_up, x_down, y_up, y_down, z_up, z_down):
        return (
            lax.ppermute(x_up, "gx", line("gx", 1)).reshape(8, 96, 128),
            lax.ppermute(x_down, "gx", line("gx", -1)).reshape(8, 96, 128),
            lax.ppermute(y_up, "gy", line("gy", 1)).reshape(8, 128, 128),
            lax.ppermute(y_down, "gy", line("gy", -1)).reshape(8, 128, 128),
            lax.ppermute(z_up, "gz", line("gz", 1)),
            lax.ppermute(z_down, "gz", line("gz", -1)),
        )

    def stencil(value, edges, extra=()):
        args = (orbital_shift, value, *edges, pot, *bands, *extra)
        outs = (shape(8, 256, 128), shape(256, 128)) if extra else shape(8, 256, 128)
        kernel = functools.partial(stencil_kernel, bool(extra))
        return call(kernel, "stencil", args, outs, flops=1 << 30, moved=6 << 20)

    def project(value, first=0, last=5, *before):
        counts, start = PIECES[first:last], sum(PIECES[:first])
        args = (ids, value.reshape(2048, 128), *pieces[first:last], ones, *before)
        scratch = [LINE_SCRATCH, pltpu.VMEM((32 * sum(counts), 128), F32)]
        kernel = functools.partial(project_kernel, counts, start)
        return call(kernel, "project", args, shape(4, 512), scratch, flops=1 << 30, moved=5 << 20)

    def place(sums, outs, extra=()):
        args = (ids, sums, *beside(sums), couplings, *pieces, ones, *extra)
        scratch = [ATOM_SCRATCH, LINE_SCRATCH]
        kernel = functools.partial(place_kernel, bool(extra))
        return call(kernel, "place", args, outs, scratch, flops=1 << 30, moved=7 << 20)

    z_edge = shape(8, 2048)
    edges = call(z_faces_kernel, "z_faces", (b.reshape(2048, 128), pick), (z_edge, z_edge), scalars=0)
    edges = halos(
        right_side[:, 10:], right_side[:, :6], right_side[:, :, 8:], right_side[:, :, :8], *edges
    )
    local = stencil(b, edges)
    x_edge, y_edge = shape(8, 96, 128), shape(8, 128, 128)
    outs = (shape(2048, 128), x_edge, x_edge, y_edge, y_edge, z_edge, z_edge, shape(8, 128))
    sums = project(b, 3, 5, project(b, 0, 3))
    w1, *edges, moments = place(sums, outs, (local.reshape(2048, 128), b.reshape(2048, 128), pick))
    edges = halos(*edges)
    added = place(project(w1), shape(2048, 128)).reshape(8, 256, 128)
    w1 = w1.reshape(8, 256, 128)
    w2, moments = stencil(w1, edges, (added, moments))
    moments = lax.all_to_all(moments, GRID, 0, 0, tiled=True)
    outs = (shape(8, 256, 128), shape(8, 256, 128))
    solved, residual = call(finish_kernel, "finish", (moments, b, w1, w2), outs, scalars=0, moved=5 << 20)
    return solved.reshape(right_side.shape), residual.reshape(right_side.shape)


def solution(mesh):
    field = P(None, *GRID)
    atoms = (P(GRID, None, None, None), P(GRID, None), P(GRID, None))
    return jax.shard_map(
        on_device,
        mesh=mesh,
        in_specs=(field, P(*GRID), P(), *atoms),
        out_specs=(field, field),
        check_vma=False,
    )
```

```python
import functools

import jax
import jax.numpy as jnp
import numpy as np
from jax import lax
from jax.experimental import pallas as pl
from jax.experimental.pallas import tpu as pltpu
from jax.sharding import PartitionSpec as P


STENCIL = (
    -5369.0 / 1800.0,
    12.0 / 7.0,
    -15.0 / 56.0,
    10.0 / 189.0,
    -1.0 / 112.0,
    2.0 / 1925.0,
    -1.0 / 16632.0,
)
GRID = ("gx", "gy", "gz")
F32 = jnp.float32
BF16 = jnp.bfloat16
VM = pl.BlockSpec(memory_space=pltpu.VMEM)
SM = pl.BlockSpec(memory_space=pltpu.SMEM)
NN = (((1,), (0,)), ((), ()))
NT = (((1,), (1,)), ((), ()))
TN = (((0,), (0,)), ((), ()))

PIECES = (16, 16, 16, 8, 8)
OFFSETS = (0, -1, 1, 2)


def slot_of(offset):
    return {0: 0, 3: 1, 1: 2, 2: 3}[offset % 4]


def weight(step):
    step = abs(step)
    return -0.5 * STENCIL[step] if 0 < step <= 6 else 0.0


def plane_matrix():
    mat = np.zeros((256, 704))
    for x in range(16):
        for y in range(16):
            row = x * 16 + y
            mat[row, row] = -0.5 * 3.0 * STENCIL[0]
            for reach in range(1, 7):
                for step in (reach, -reach):
                    to_x, to_y = x + step, y + step
                    if 0 <= to_x < 16:
                        mat[row, to_x * 16 + y] += weight(reach)
                    elif to_x < 0:
                        mat[row, 256 + (to_x + 6) * 16 + y] += weight(reach)
                    else:
                        mat[row, 352 + (to_x - 16) * 16 + y] += weight(reach)
                    if 0 <= to_y < 16:
                        mat[row, x * 16 + to_y] += weight(reach)
                    elif to_y < 0:
                        mat[row, 448 + x * 8 + (to_y + 8)] += weight(reach)
                    else:
                        mat[row, 576 + x * 8 + (to_y - 16)] += weight(reach)
    return mat


def z_matrix():
    mat = np.zeros((128, 128))
    for z in range(128):
        for step in range(-6, 7):
            if 0 <= z + step < 128:
                mat[z + step, z] += weight(step)
    return mat


def z_halo_matrix():
    mat = np.zeros((16, 128))
    for z in range(128):
        for reach in range(1, 7):
            if z - reach < 0:
                mat[z - reach + 6, z] += weight(reach)
            if z + reach >= 128:
                mat[8 + z + reach - 128, z] += weight(reach)
    return mat


def pick_matrix():
    mat = np.zeros((16, 128))
    for cell in range(6):
        mat[cell, 122 + cell] = 1.0
        mat[8 + cell, cell] = 1.0
    return mat


def two_parts(mat):
    high = mat.astype(np.float32).astype(BF16)
    low = (mat - high.astype(np.float64)).astype(np.float32).astype(BF16)
    return high, low


def constants():
    plane = two_parts(plane_matrix())
    z_band = np.concatenate(two_parts(z_matrix()))
    z_halo = np.concatenate(two_parts(z_halo_matrix()))
    pick = pick_matrix().astype(np.float32).astype(BF16)
    ones = np.ones((16, 128), np.float32).astype(BF16)
    return tuple(jnp.asarray(part) for part in (*plane, z_band, z_halo, pick, ones))


def dot(lhs, rhs, dims):
    return lax.dot_general(lhs, rhs, dims, preferred_element_type=F32)


def split2(value):
    high = value.astype(BF16)
    return high, (value - high.astype(F32)).astype(BF16)


def split3(value):
    high = value.astype(BF16)
    rest = value - high.astype(F32)
    mid = rest.astype(BF16)
    return high, mid, (rest - mid.astype(F32)).astype(BF16)


def iota(shape, dim):
    return lax.broadcasted_iota(jnp.int32, shape, dim)


def z_faces(value, pick):
    high, mid, low = split3(value)
    return dot(pick, high, NT) + dot(pick, mid, NT) + dot(pick, low, NT)


def z_faces_kernel(v_ref, pick_ref, up_ref, down_ref):
    faces = z_faces(v_ref[...], pick_ref[...])
    up_ref[...] = faces[:8]
    down_ref[...] = faces[8:]


def z_face(ref):
    return jnp.concatenate([ref[16 + i * 8 : 24 + i * 8, :] for i in range(16)], axis=1)


def sums_at(r, here, lower, upper, opposite):
    rows = []
    for q in range(4):
        total = here[r * 4 + q : r * 4 + q + 1, :]
        for ref, away in ((lower, -1), (upper, 1), (opposite, 2)):
            at = slot_of(OFFSETS[r] - away) * 4 + q
            total = total + ref[at : at + 1, :]
        rows.append(total)
    return jnp.concatenate(rows, axis=1)


def own_form(sums, coupling):
    terms = coupling * sums * sums
    terms = (terms[:, :128] + terms[:, 128:256]) + (terms[:, 256:384] + terms[:, 384:])
    terms = jnp.broadcast_to(terms, (8, 128))
    for step in (64, 32, 16, 8):
        terms = terms + pltpu.roll(terms, step, axis=1)
    lane = iota((8, 128), 1)
    return jnp.where((lane >= 24) & (lane < 32), terms, 0.0)[0:1]


def stencil_kernel(last, shift_ref, *rest):
    if last:
        inside_ref, *rest = rest
    v_ref, xl, xh, yl, yh, zl, zh, pot, kh_ref, kl_ref, zb_ref, zc_ref, *rest = rest
    if last:
        here, opposite, coupling_ref, moment_ref, out_ref, sent_ref = rest
        edges = [z_face(zl) * inside_ref[0], z_face(zh) * inside_ref[1]]
    else:
        (out_ref,) = rest
        edges = [zl[...], zh[...]]
    plane_high, plane_low = kh_ref[...], kl_ref[...]
    edge_high, edge_low = split2(jnp.concatenate(edges, axis=0))
    z_halo, z_band = zc_ref[...], zb_ref[...]
    lane, row = iota((8, 128), 1), iota((8, 128), 0)
    moment = jnp.zeros((8, 128), F32)
    for first in range(0, 8, 2):
        pair = (first, first + 1)
        columns = [jnp.concatenate([v_ref[n], xl[n], xh[n], yl[n], yh[n]], axis=0) for n in pair]
        high, low = split2(jnp.concatenate(columns, axis=1))
        plane = dot(plane_high, high, NN) + dot(plane_high, low, NN) + dot(plane_low, high, NN)
        for i, n in enumerate(pair):
            lanes = slice(i * 128, (i + 1) * 128)
            own_high, own_low = high[:256, lanes], low[:256, lanes]
            out = plane[:, lanes] + dot(own_high, z_band[:128], NN)
            out = out + dot(own_low, z_band[:128], NN) + dot(own_high, z_band[128:], NN)
            above, below = edge_high[:, n * 256 : (n + 1) * 256], edge_low[:, n * 256 : (n + 1) * 256]
            out = out + dot(above, z_halo[:16], TN) + dot(below, z_halo[:16], TN) + dot(above, z_halo[16:], TN)
            value = v_ref[n]
            out = out + (pot[...] + shift_ref[n]) * value
            if last:
                moment = jnp.where((lane == 3) & (row == n), jnp.sum(value * out), moment)
            out_ref[n] = out
    if last:
        moment = moment + moment_ref[...]
        flat = jnp.zeros((8, 128), F32)
        for i in range(4):
            flat = flat + jnp.where(lane == i * 8 + row, moment[:, i : i + 1], 0.0)
        flat = jnp.sum(flat, axis=0, keepdims=True)
        flat = flat + own_form(sums_at(0, here, zl, zh, opposite), coupling_ref[0:1, :])
        sent_ref[...] = jnp.broadcast_to(flat, sent_ref.shape)


def to_lines(src, dst):
    def eight(i, carry):
        for u in range(8):
            line = i * 8 + u
            dst[line] = src[pl.ds(line, 8, stride=256), :]
        return carry

    lax.fori_loop(0, 32, eight, 0)


def project_lines(ids_ref, pieces, counts, start, lines, sums_ref, ones):
    base = start
    for ref, count in zip(pieces, counts):

        def atom(a, carry, ref=ref, base=base):
            sums = [jnp.zeros((8, 128), F32) for _ in range(4)]
            for k in range(32):
                value = lines[ids_ref[(base + a) * 32 + k]]
                for j in range(4):
                    sums[j] = sums[j] + value * ref[pl.ds((a * 4 + j) * 32 + k, 8, stride=0), :]
            for j in range(4):
                sums_ref[pl.ds(pl.multiple_of(((base - start + a) * 4 + j) * 8, 8), 8), :] = sums[j]
            return carry

        lax.fori_loop(0, count, atom, 0)
        base += count
    high, mid, low = split3(sums_ref[...])
    return dot(ones, high, NT) + dot(ones, mid, NT) + dot(ones, low, NT)


def store_rows(total, first, out_refs):
    for row in range(total.shape[1] // 128):
        for ref in out_refs:
            ref[first + row : first + row + 1, :] = total[0:1, row * 128 : (row + 1) * 128]


def project_kernel(counts, start, ids_ref, v_ref, *rest):
    pieces, rest = rest[: len(counts)], rest[len(counts) :]
    ones_ref, *before, out_ref, lines, sums_ref = rest
    to_lines(v_ref, lines)
    lines[256] = jnp.zeros((8, 128), F32)
    total = project_lines(ids_ref, pieces, counts, start, lines, sums_ref, ones_ref[...])
    if before:
        out_ref[...] = before[0][...]
    store_rows(total, start // 4, (out_ref,))


def place_kernel(first, ids_ref, here, lower, upper, opposite, coupling_ref, *rest):
    pieces, (ones_ref, base_ref) = rest[:5], rest[5:7]
    if first:
        b_ref, pick_ref = rest[7:9]
        out_ref, x_up, x_down, y_up, y_down, up_ref, down_ref, moment_ref, weights, lines = rest[9:]
    else:
        out_ref, weights, lines = rest[7:]
    ones = ones_ref[...]
    rows = [sums_at(r, here, lower, upper, opposite) * coupling_ref[r : r + 1, :] for r in range(4)]
    high, mid, low = (part.astype(F32) for part in split3(jnp.concatenate(rows, axis=1)))
    row = iota((16, 2048), 0)
    stacked = jnp.where(row == 0, high, jnp.where(row == 1, mid, jnp.where(row == 2, low, 0.0)))
    weights[...] = dot(stacked.astype(BF16), ones, TN)
    to_lines(base_ref, lines)
    base = 0
    for ref, count in zip(pieces, PIECES):

        def atom(a, carry, ref=ref, base=base):
            of = [weights[pl.ds(pl.multiple_of(((base + a) * 4 + j) * 8, 8), 8), :] for j in range(4)]
            for chunk in range(4):
                at = [ids_ref[(base + a) * 32 + chunk * 8 + k] for k in range(8)]
                values = [lines[line] for line in at]
                for k in range(8):
                    terms = [
                        of[j] * ref[pl.ds((a * 4 + j) * 32 + chunk * 8 + k, 8, stride=0), :] for j in range(4)
                    ]
                    values[k] = values[k] + ((terms[0] + terms[1]) + (terms[2] + terms[3]))
                for k in range(8):
                    lines[at[k]] = values[k]
            return carry

        lax.fori_loop(0, count, atom, 0)
        base += count
    if not first:

        def back(i, carry):
            for u in range(8):
                line = i * 8 + u
                out_ref[pl.ds(line, 8, stride=256), :] = lines[line]
            return carry

        lax.fori_loop(0, 32, back, 0)
        return

    def finish(i, moments):
        m0, m1, m2 = moments
        for u in range(8):
            line = i * 8 + u
            image, value = lines[line], b_ref[pl.ds(line, 8, stride=256), :]
            out_ref[pl.ds(line, 8, stride=256), :] = image
            m0, m1, m2 = m0 + value * value, m1 + value * image, m2 + image * image
        return m0, m1, m2

    zero = jnp.zeros((8, 128), F32)
    moments = lax.fori_loop(0, 32, finish, (zero, zero, zero))
    lane = iota((8, 128), 1)
    stored = zero
    for i in range(3):
        stored = jnp.where(lane == i, jnp.sum(moments[i], axis=1, keepdims=True), stored)
    moment_ref[...] = stored
    lines[256] = zero
    total = project_lines(ids_ref, pieces, PIECES, 0, lines, weights, ones)
    store_rows(total, 0, (up_ref, down_ref))
    image = out_ref[...]
    faces = z_faces(image, pick_ref[...])
    for i in range(16):
        up_ref[16 + i * 8 : 24 + i * 8, :] = faces[:8, i * 128 : (i + 1) * 128]
        down_ref[16 + i * 8 : 24 + i * 8, :] = faces[8:, i * 128 : (i + 1) * 128]
    by_x = image.reshape(8, 256, 128)
    x_up[...] = by_x[:, 160:]
    x_down[...] = by_x[:, :96]
    by_y = image.reshape(128, 2, 8, 128)
    y_up[...] = by_y[:, 1].reshape(8, 128, 128)
    y_down[...] = by_y[:, 0].reshape(8, 128, 128)


def finish_kernel(moments_ref, b_ref, w1_ref, w2_ref, solution_ref, residual_ref):
    flat = jnp.sum(moments_ref[...], axis=0, keepdims=True)
    m0, m1, m2, m3 = (flat[:, i * 8 : (i + 1) * 8] for i in range(4))
    alpha = m0 / m1
    fresh = alpha * (alpha * m2 - 2.0 * m1) + m0
    product = m1 + alpha * (alpha * m3 - 2.0 * m2)
    beta = fresh / m0
    alpha2 = fresh / (product - beta * fresh / alpha)
    s1 = alpha + alpha2 * (1.0 + beta)
    s2 = alpha * alpha2
    for n in range(8):
        one, two = s1[:, n : n + 1], s2[:, n : n + 1]
        b, w1, w2 = b_ref[n], w1_ref[n], w2_ref[n]
        solution_ref[n] = one * b - two * w1
        residual_ref[n] = b - one * w1 + two * w2


def shape(*dims):
    return jax.ShapeDtypeStruct(dims, F32)


def call(kernel, name, args, outs, scratch=(), scalars=1, flops=0, moved=1 << 20):
    many = isinstance(outs, tuple)
    return pl.pallas_call(
        kernel,
        out_shape=outs,
        in_specs=[SM] * scalars + [VM] * (len(args) - scalars),
        out_specs=(VM,) * len(outs) if many else VM,
        scratch_shapes=scratch,
        name=name,
        cost_estimate=pl.CostEstimate(flops=flops, bytes_accessed=moved, transcendentals=0),
    )(*args)


LINE_SCRATCH = pltpu.VMEM((264, 8, 128), F32)
ATOM_SCRATCH = pltpu.VMEM((2048, 128), F32)


def on_device(right_side, potential, orbital_shift, projector, coupling, block_ids):
    plane_high, plane_low, z_band, z_halo, pick, ones = constants()
    bands = (plane_high, plane_low, z_band, z_halo)
    b = right_side.reshape(8, 256, 128)
    pot = potential.reshape(256, 128)
    own = projector.reshape(2048, 128)
    around = {shift: [(i, (i + shift) % 4) for i in range(4)] for shift in (1, -1, 2)}

    def beside(array):
        return tuple(lax.ppermute(array, "gz", around[shift]) for shift in (1, -1, 2))

    lower = lax.ppermute(own, "gz", around[1])
    upper = lax.ppermute(own, "gz", around[-1])
    pieces = (
        own,
        lower,
        upper,
        lax.ppermute(lower[:1024], "gz", around[1]),
        lax.ppermute(upper[1024:], "gz", around[-1]),
    )
    side = jnp.concatenate(
        [block_ids.astype(F32).reshape(512), coupling.reshape(64), jnp.zeros((448,), F32)]
    ).reshape(8, 128)
    sides = jnp.stack((side, *beside(side)))
    ids = sides[:, :4].reshape(2048).astype(jnp.int32) - 256 * lax.axis_index("gz")
    ids = jnp.where((ids >= 0) & (ids < 256), ids, 256)
    couplings = jnp.repeat(sides[:, 4, :64], 8, axis=1)

    def line(axis, step):
        size = lax.axis_size(axis)
        return [(i, i + step) for i in range(size) if 0 <= i + step < size]

    def halos(x_up, x_down, y_up, y_down):
        return (
            lax.ppermute(x_up, "gx", line("gx", 1)).reshape(8, 96, 128),
            lax.ppermute(x_down, "gx", line("gx", -1)).reshape(8, 96, 128),
            lax.ppermute(y_up, "gy", line("gy", 1)).reshape(8, 128, 128),
            lax.ppermute(y_down, "gy", line("gy", -1)).reshape(8, 128, 128),
        )

    def project(value, first=0, last=5, *before):
        counts, start = PIECES[first:last], sum(PIECES[:first])
        args = (ids, value.reshape(2048, 128), *pieces[first:last], ones, *before)
        scratch = [LINE_SCRATCH, pltpu.VMEM((32 * sum(counts), 128), F32)]
        kernel = functools.partial(project_kernel, counts, start)
        return call(kernel, "project", args, shape(16, 128), scratch, flops=1 << 30, moved=5 << 20)

    def place(sums, outs, *extra):
        args = (ids, *sums, couplings, *pieces, ones, *extra)
        scratch = [ATOM_SCRATCH, LINE_SCRATCH]
        kernel = functools.partial(place_kernel, len(extra) > 1)
        return call(kernel, "place", args, outs, scratch, flops=1 << 32, moved=7 << 20)

    z_edge = shape(8, 2048)
    z_up, z_down = call(z_faces_kernel, "z_faces", (b.reshape(2048, 128), pick), (z_edge, z_edge), scalars=0)
    edges = halos(right_side[:, 10:], right_side[:, :6], right_side[:, :, 8:], right_side[:, :, :8])
    z_low = lax.ppermute(z_up, "gz", line("gz", 1))
    z_high = lax.ppermute(z_down, "gz", line("gz", -1))
    args = (orbital_shift, b, *edges, z_low, z_high, pot, *bands)
    kernel = functools.partial(stencil_kernel, False)
    local = call(kernel, "stencil", args, shape(8, 256, 128), flops=1 << 30, moved=6 << 20)
    sums = project(b, 3, 5, project(b, 0, 3))
    x_edge, y_edge, packed = shape(8, 96, 128), shape(8, 128, 128), shape(144, 128)
    outs = (shape(2048, 128), x_edge, x_edge, y_edge, y_edge, packed, packed, shape(8, 128))
    extra = (local.reshape(2048, 128), b.reshape(2048, 128), pick)
    w1, *edges, up, down, moments = place((sums, *beside(sums)), outs, *extra)

    opposite = lax.ppermute(up[:16], "gz", around[2])
    lower = lax.ppermute(up, "gz", around[1])
    upper = lax.ppermute(down, "gz", around[-1])
    edges = halos(*edges)
    w1 = w1.reshape(8, 256, 128)
    column = lax.axis_index("gz")
    inside = jnp.stack([column > 0, column < lax.axis_size("gz") - 1]).astype(F32)
    args = (orbital_shift, inside, w1, *edges, lower, upper, pot, *bands, up, opposite, couplings, moments)
    outs = (shape(8, 256, 128), shape(256, 128))
    kernel = functools.partial(stencil_kernel, True)
    local, moments = call(kernel, "stencil", args, outs, scalars=2, flops=1 << 30, moved=6 << 20)
    moments = lax.all_to_all(moments, GRID, 0, 0, tiled=True)
    w2 = place((up, lower, upper, opposite), shape(2048, 128), local.reshape(2048, 128))
    args = (moments, b, w1, w2.reshape(8, 256, 128))
    outs = (shape(8, 256, 128), shape(8, 256, 128))
    solved, residual = call(finish_kernel, "finish", args, outs, scalars=0, moved=5 << 20)
    return solved.reshape(right_side.shape), residual.reshape(right_side.shape)


def solution(mesh):
    field = P(None, *GRID)
    atoms = (P(GRID, None, None, None), P(GRID, None), P(GRID, None))
    return jax.shard_map(
        on_device,
        mesh=mesh,
        in_specs=(field, P(*GRID), P(), *atoms),
        out_specs=(field, field),
        check_vma=False,
    )
```

```python
import functools

import jax
import jax.numpy as jnp
import numpy as np
from jax import lax
from jax.experimental import pallas as pl
from jax.experimental.pallas import tpu as pltpu
from jax.sharding import PartitionSpec as P


STENCIL = (
    -5369.0 / 1800.0,
    12.0 / 7.0,
    -15.0 / 56.0,
    10.0 / 189.0,
    -1.0 / 112.0,
    2.0 / 1925.0,
    -1.0 / 16632.0,
)
GRID = ("gx", "gy", "gz")
F32 = jnp.float32
BF16 = jnp.bfloat16
VM = pl.BlockSpec(memory_space=pltpu.VMEM)
SM = pl.BlockSpec(memory_space=pltpu.SMEM)
NN = (((1,), (0,)), ((), ()))
NT = (((1,), (1,)), ((), ()))
TN = (((0,), (0,)), ((), ()))

OFFSETS = (0, -1, 1, 2)
SLOTS, MOST, BATCH = 200, 188, 12
LIST, FLAG = 32, 20
ROWS = SLOTS * 4


def slot_of(offset):
    return {0: 0, 3: 1, 1: 2, 2: 3}[offset % 4]


def weight(step):
    step = abs(step)
    return -0.5 * STENCIL[step] if 0 < step <= 6 else 0.0


def plane_matrix():
    mat = np.zeros((256, 704))
    for x in range(16):
        for y in range(16):
            row = x * 16 + y
            mat[row, row] = -0.5 * 3.0 * STENCIL[0]
            for reach in range(1, 7):
                for step in (reach, -reach):
                    to_x, to_y = x + step, y + step
                    if 0 <= to_x < 16:
                        mat[row, to_x * 16 + y] += weight(reach)
                    elif to_x < 0:
                        mat[row, 256 + (to_x + 6) * 16 + y] += weight(reach)
                    else:
                        mat[row, 352 + (to_x - 16) * 16 + y] += weight(reach)
                    if 0 <= to_y < 16:
                        mat[row, x * 16 + to_y] += weight(reach)
                    elif to_y < 0:
                        mat[row, 448 + x * 8 + (to_y + 8)] += weight(reach)
                    else:
                        mat[row, 576 + x * 8 + (to_y - 16)] += weight(reach)
    return mat


def z_matrix():
    mat = np.zeros((128, 128))
    for z in range(128):
        for step in range(-6, 7):
            if 0 <= z + step < 128:
                mat[z + step, z] += weight(step)
    return mat


def z_halo_matrix():
    mat = np.zeros((16, 128))
    for z in range(128):
        for reach in range(1, 7):
            if z - reach < 0:
                mat[z - reach + 6, z] += weight(reach)
            if z + reach >= 128:
                mat[8 + z + reach - 128, z] += weight(reach)
    return mat


def pick_matrix():
    mat = np.zeros((16, 128))
    for cell in range(6):
        mat[cell, 122 + cell] = 1.0
        mat[8 + cell, cell] = 1.0
    return mat


def two_parts(mat):
    high = mat.astype(np.float32).astype(BF16)
    low = (mat - high.astype(np.float64)).astype(np.float32).astype(BF16)
    return high, low


def constants():
    plane = two_parts(plane_matrix())
    z_band = np.concatenate(two_parts(z_matrix()))
    z_halo = np.concatenate(two_parts(z_halo_matrix()))
    pick = pick_matrix().astype(np.float32).astype(BF16)
    return tuple(jnp.asarray(part) for part in (*plane, z_band, z_halo, pick))


def dot(lhs, rhs, dims):
    return lax.dot_general(lhs, rhs, dims, preferred_element_type=F32)


def split2(value):
    high = value.astype(BF16)
    return high, (value - high.astype(F32)).astype(BF16)


def split3(value):
    high = value.astype(BF16)
    rest = value - high.astype(F32)
    mid = rest.astype(BF16)
    return high, mid, (rest - mid.astype(F32)).astype(BF16)


def iota(shape, dim):
    return lax.broadcasted_iota(jnp.int32, shape, dim)


def z_faces(value, pick):
    high, mid, low = split3(value)
    return dot(pick, high, NT) + dot(pick, mid, NT) + dot(pick, low, NT)


def pack_kernel(column_ref, ids_ref, own_ref, coupling_ref, v_ref, pick_ref, *rest):
    here_ref, up_ref, opposite_ref, down_ref, *rest = rest
    out_lists, faces_out, (lists_ref, packed, counts, scale_ref, face_done, list_done) = rest[:4], rest[4:8], rest[8:]
    parts = (
        v_ref.at[:, pl.ds(10, 6)],
        v_ref.at[:, pl.ds(0, 6)],
        v_ref.at[:, :, pl.ds(8, 8)],
        v_ref.at[:, :, pl.ds(0, 8)],
    )
    copies = [pltpu.make_async_copy(part, out, face_done.at[i]) for i, (part, out) in enumerate(zip(parts, faces_out))]
    for copy in copies:
        copy.start()
    root = jnp.sqrt(coupling_ref[...])
    for a in range(16):
        scale_ref[a * 4 : a * 4 + 4, :] = jnp.broadcast_to(root[:, a : a + 1], (4, 128))
    for dest in range(4):
        counts[dest] = 0
    packed[...] = jnp.zeros_like(packed)
    column = column_ref[0]

    def atom(a, carry):
        for dest in range(4):
            lists_ref[dest * 256 + a] = counts[dest]
        scale = scale_ref[pl.ds(pl.multiple_of(a * 4, 4), 4), :]
        for k in range(32):
            block = ids_ref[a, k]
            dest = (jnp.right_shift(block, 8) - column) & 3
            taken = counts[dest]
            counts[dest] = taken + 1
            slot = jnp.minimum(taken, SLOTS - 1)
            lists_ref[dest * 256 + LIST + slot] = block & 255
            rows = own_ref[pl.ds(a * 128 + k, 4, stride=32), :] * scale
            packed[pl.ds(pl.multiple_of((dest * SLOTS + slot) * 4, 4), 4), :] = rows
        return carry

    lax.fori_loop(0, 16, atom, 0)
    most = jnp.maximum(jnp.maximum(counts[0], counts[1]), jnp.maximum(counts[2], counts[3]))
    over = (most > MOST).astype(jnp.int32)
    for dest in range(4):
        lists_ref[dest * 256 + 16] = counts[dest]
        lists_ref[dest * 256 + FLAG] = over
    for dest in range(4):
        part = lists_ref.at[pl.ds(dest * 256, 256)]
        copies.append(pltpu.make_async_copy(part, out_lists[dest], list_done.at[dest]))
        copies[-1].start()
    faces = z_faces(v_ref[...].reshape(2048, 128), pick_ref[...])
    for i in range(16):
        up_ref[i * 8 : i * 8 + 8, :] = faces[:8, i * 128 : (i + 1) * 128]
        down_ref[i * 8 : i * 8 + 8, :] = faces[8:, i * 128 : (i + 1) * 128]
    here_ref[...] = packed[:ROWS, :]
    up_ref[128:, :] = packed[ROWS : 2 * ROWS, :]
    opposite_ref[...] = packed[2 * ROWS : 3 * ROWS, :]
    down_ref[128:, :] = packed[3 * ROWS :, :]
    for copy in copies:
        copy.wait()


def over_kernel(lists0, lists1, lists2, lists3, out_ref):
    out_ref[0] = overflow((lists0, lists1, lists2, lists3))


def nothing_kernel(out_ref, ids_ref):
    del out_ref, ids_ref


def z_face(ref, start):
    return jnp.concatenate([ref[start + i * 8 : start + i * 8 + 8, :] for i in range(16)], axis=1)


def sums_at(r, here, lower, upper, opposite):
    rows = []
    for q in range(4):
        total = here[r * 4 + q : r * 4 + q + 1, :]
        for ref, away in ((lower, -1), (upper, 1), (opposite, 2)):
            at = slot_of(OFFSETS[r] - away) * 4 + q
            total = total + ref[at : at + 1, :]
        rows.append(total)
    return jnp.concatenate(rows, axis=1)


def own_form(sums):
    terms = sums * sums
    terms = (terms[:, :128] + terms[:, 128:256]) + (terms[:, 256:384] + terms[:, 384:])
    terms = jnp.broadcast_to(terms, (8, 128))
    for step in (64, 32, 16, 8):
        terms = terms + pltpu.roll(terms, step, axis=1)
    lane = iota((8, 128), 1)
    return jnp.where((lane >= 24) & (lane < 32), terms, 0.0)[0:1]


def stencil_kernel(last, size, shift_ref, column_ref, v_ref, xl, xh, yl, yh, zl, zh, pot, *rest):
    kh_ref, kl_ref, zb_ref, zc_ref, *rest = rest
    if last:
        here, opposite, moment_ref, out_ref, sent_ref = rest
    else:
        (out_ref,) = rest
    start = 16 if last else 0
    below = (column_ref[0] > 0).astype(F32)
    above = (column_ref[0] < size - 1).astype(F32)
    edges = [z_face(zl, start) * below, z_face(zh, start) * above]
    plane_high, plane_low = kh_ref[...], kl_ref[...]
    edge_high, edge_low = split2(jnp.concatenate(edges, axis=0))
    z_halo, z_band = zc_ref[...], zb_ref[...]
    lane, row = iota((8, 128), 1), iota((8, 128), 0)
    moment = jnp.zeros((8, 128), F32)
    for first in range(0, 8, 2):
        pair = (first, first + 1)
        columns = [jnp.concatenate([v_ref[n], xl[n], xh[n], yl[n], yh[n]], axis=0) for n in pair]
        high, low = split2(jnp.concatenate(columns, axis=1))
        plane = dot(plane_high, high, NN) + dot(plane_high, low, NN) + dot(plane_low, high, NN)
        for i, n in enumerate(pair):
            lanes = slice(i * 128, (i + 1) * 128)
            own_high, own_low = high[:256, lanes], low[:256, lanes]
            out = plane[:, lanes] + dot(own_high, z_band[:128], NN)
            out = out + dot(own_low, z_band[:128], NN) + dot(own_high, z_band[128:], NN)
            rows = slice(n * 256, (n + 1) * 256)
            faces_high, faces_low = edge_high[:, rows], edge_low[:, rows]
            out = out + dot(faces_high, z_halo[:16], TN) + dot(faces_low, z_halo[:16], TN)
            out = out + dot(faces_high, z_halo[16:], TN)
            value = v_ref[n]
            out = out + (pot[...] + shift_ref[n]) * value
            if last:
                moment = jnp.where((lane == 3) & (row == n), jnp.sum(value * out), moment)
            out_ref[n] = out
    if last:
        moment = moment + moment_ref[...]
        flat = jnp.zeros((8, 128), F32)
        for i in range(4):
            flat = flat + jnp.where(lane == i * 8 + row, moment[:, i : i + 1], 0.0)
        flat = jnp.sum(flat, axis=0, keepdims=True)
        flat = flat + own_form(sums_at(0, here, zl, zh, opposite))
        sent_ref[...] = jnp.broadcast_to(flat, sent_ref.shape)


def to_lines(src, dst):
    def eight(i, carry):
        for u in range(8):
            line = i * 8 + u
            dst[line] = src[pl.ds(line, 8, stride=256), :]
        return carry

    lax.fori_loop(0, 32, eight, 0)


def overflow(lists):
    return (lists[0][FLAG] | lists[1][FLAG]) | (lists[2][FLAG] | lists[3][FLAG])


def from_all(all_ref, buffer, done, visit):
    def owner(r, carry):
        rows = pl.ds(pl.multiple_of(r * 2048, 2048), 2048)
        copy = pltpu.make_async_copy(all_ref.at[rows, :], buffer, done)
        copy.start()
        copy.wait()
        lax.fori_loop(0, 16, functools.partial(visit, r), 0)
        return carry

    lax.fori_loop(0, 4, owner, 0)


def weight_rows(r, a, j):
    return pl.ds(pl.multiple_of(((r * 16 + a) * 4 + j) * 8, 8), 8)


def batch_of(lists, start, end, size):
    slots = [start + k for k in range(size)]
    return slots, [jnp.where(slot < end, lists[LIST + slot], 256) for slot in slots]


def project_lines(spheres, lines, sums_ref):
    lists, ids_ref, pieces, skips, all_ref, buffer, done = spheres
    over = overflow(lists)

    def add(r, a, sums, slots, at):
        for slot, line in zip(slots, at):
            value = lines[line]
            for j in range(4):
                sums[j] = sums[j] + value * pieces[r][pl.ds(skips[r] + slot * 4 + j, 8, stride=0), :]
        for j in range(4):
            sums_ref[weight_rows(r, a, j), :] = sums[j]

    @pl.when(over == 0)
    def _():
        for r in range(4):

            def atom(a, carry, r=r):
                start, end = lists[r][a], lists[r][a + 1]
                add(r, a, [jnp.zeros((8, 128), F32) for _ in range(4)], *batch_of(lists[r], start, end, BATCH))
                return carry

            def rest(a, carry, r=r):
                start, end = lists[r][a] + BATCH, lists[r][a + 1]

                def four(i, carry):
                    sums = [sums_ref[weight_rows(r, a, j), :] for j in range(4)]
                    add(r, a, sums, *batch_of(lists[r], start + i * 4, end, 4))
                    return carry

                return lax.fori_loop(0, jnp.right_shift(end - start + 3, 2), four, carry)

            lax.fori_loop(0, 16, atom, 0, unroll=2)
            lax.fori_loop(0, 16, rest, 0)

    @pl.when(over != 0)
    def _():
        def visit(r, a, carry):
            sums = [jnp.zeros((8, 128), F32) for _ in range(4)]
            for k in range(32):
                value = lines[ids_ref[(r * 16 + a) * 32 + k]]
                for j in range(4):
                    sums[j] = sums[j] + value * buffer[pl.ds((a * 4 + j) * 32 + k, 8, stride=0), :]
            for j in range(4):
                sums_ref[weight_rows(r, a, j), :] = sums[j]
            return carry

        from_all(all_ref, buffer, done, visit)

    high, mid, low = split3(sums_ref[...])
    ones = jnp.ones((16, 128), BF16)
    return dot(ones, high, NT) + dot(ones, mid, NT) + dot(ones, low, NT)


def place_lines(spheres, lines, weights):
    lists, ids_ref, pieces, skips, all_ref, buffer, done = spheres
    over = overflow(lists)

    def add(of, at, rows):
        values = [lines[line] for line in at]
        for k in range(len(at)):
            terms = [of[j] * rows(k, j) for j in range(4)]
            values[k] = values[k] + ((terms[0] + terms[1]) + (terms[2] + terms[3]))
        for k in range(len(at)):
            lines[at[k]] = values[k]

    @pl.when(over == 0)
    def _():
        for r in range(4):

            def some(a, start, end, size, r=r):
                slots, at = batch_of(lists[r], start, end, size)
                of = [weights[weight_rows(r, a, j), :] for j in range(4)]
                add(of, at, lambda k, j: pieces[r][pl.ds(skips[r] + slots[k] * 4 + j, 8, stride=0), :])

            def atom(a, carry, r=r, some=some):
                some(a, lists[r][a], lists[r][a + 1], BATCH)
                return carry

            def rest(a, carry, r=r, some=some):
                start, end = lists[r][a] + BATCH, lists[r][a + 1]

                def four(i, carry):
                    some(a, start + i * 4, end, 4)
                    return carry

                return lax.fori_loop(0, jnp.right_shift(end - start + 3, 2), four, carry)

            lax.fori_loop(0, 16, atom, 0, unroll=2)
            lax.fori_loop(0, 16, rest, 0)

    @pl.when(over != 0)
    def _():
        def visit(r, a, carry):
            of = [weights[weight_rows(r, a, j), :] for j in range(4)]
            for chunk in range(4):
                at = [ids_ref[(r * 16 + a) * 32 + chunk * 8 + k] for k in range(8)]
                first = chunk * 8
                add(of, at, lambda k, j: buffer[pl.ds((a * 4 + j) * 32 + first + k, 8, stride=0), :])
            return carry

        from_all(all_ref, buffer, done, visit)


def sphere_refs(refs, skips, buffer, done):
    return (refs[:4], refs[4], refs[5:9], skips, refs[9], buffer, done)


def store_rows(total, first, out_refs):
    for row in range(total.shape[1] // 128):
        for ref in out_refs:
            ref[first + row : first + row + 1, :] = total[0:1, row * 128 : (row + 1) * 128]


def project_kernel(lists0, lists1, lists2, lists3, ids_ref, v_ref, *rest):
    pieces, all_ref, out_ref, lines, sums_ref, buffer, done = rest[:4], *rest[4:]
    spheres = sphere_refs((lists0, lists1, lists2, lists3, ids_ref, *pieces, all_ref), SKIPS, buffer, done)
    to_lines(v_ref, lines)
    lines[256] = jnp.zeros((8, 128), F32)
    store_rows(project_lines(spheres, lines, sums_ref), 0, (out_ref,))


def place_kernel(first, lists0, lists1, lists2, lists3, ids_ref, here, lower, upper, opposite, *rest):
    pieces, (all_ref, base_ref) = rest[:4], rest[4:6]
    *rest, weights, lines, buffer, done = rest[6:]
    if first:
        b_ref, pick_ref, out_ref, x_up, x_down, y_up, y_down, up_ref, down_ref, moment_ref = rest
    else:
        (out_ref,) = rest
    spheres = sphere_refs((lists0, lists1, lists2, lists3, ids_ref, *pieces, all_ref), SKIPS, buffer, done)
    rows = [sums_at(r, here, lower, upper, opposite) for r in range(4)]
    high, mid, low = (part.astype(F32) for part in split3(jnp.concatenate(rows, axis=1)))
    row = iota((16, 2048), 0)
    stacked = jnp.where(row == 0, high, jnp.where(row == 1, mid, jnp.where(row == 2, low, 0.0)))
    weights[...] = dot(stacked.astype(BF16), jnp.ones((16, 128), BF16), TN)
    to_lines(base_ref, lines)
    place_lines(spheres, lines, weights)
    if not first:

        def back(i, carry):
            for u in range(8):
                line = i * 8 + u
                out_ref[pl.ds(line, 8, stride=256), :] = lines[line]
            return carry

        lax.fori_loop(0, 32, back, 0)
        return

    def finish(i, moments):
        m0, m1, m2 = moments
        for u in range(8):
            line = i * 8 + u
            image, value = lines[line], b_ref[pl.ds(line, 8, stride=256), :]
            out_ref[pl.ds(line, 8, stride=256), :] = image
            m0, m1, m2 = m0 + value * value, m1 + value * image, m2 + image * image
        return m0, m1, m2

    zero = jnp.zeros((8, 128), F32)
    moments = lax.fori_loop(0, 32, finish, (zero, zero, zero))
    lane = iota((8, 128), 1)
    stored = zero
    for i in range(3):
        stored = jnp.where(lane == i, jnp.sum(moments[i], axis=1, keepdims=True), stored)
    moment_ref[...] = stored
    lines[256] = zero
    total = project_lines(spheres, lines, weights)
    store_rows(total, 0, (up_ref, down_ref))
    image = out_ref[...]
    faces = z_faces(image, pick_ref[...])
    for i in range(16):
        up_ref[16 + i * 8 : 24 + i * 8, :] = faces[:8, i * 128 : (i + 1) * 128]
        down_ref[16 + i * 8 : 24 + i * 8, :] = faces[8:, i * 128 : (i + 1) * 128]
    by_x = image.reshape(8, 256, 128)
    x_up[...] = by_x[:, 160:]
    x_down[...] = by_x[:, :96]
    by_y = image.reshape(128, 2, 8, 128)
    y_up[...] = by_y[:, 1].reshape(8, 128, 128)
    y_down[...] = by_y[:, 0].reshape(8, 128, 128)


def finish_kernel(moments_ref, b_ref, w1_ref, w2_ref, solution_ref, residual_ref):
    flat = jnp.sum(moments_ref[...], axis=0, keepdims=True)
    m0, m1, m2, m3 = (flat[:, i * 8 : (i + 1) * 8] for i in range(4))
    alpha = m0 / m1
    fresh = alpha * (alpha * m2 - 2.0 * m1) + m0
    product = m1 + alpha * (alpha * m3 - 2.0 * m2)
    beta = fresh / m0
    alpha2 = fresh / (product - beta * fresh / alpha)
    s1 = alpha + alpha2 * (1.0 + beta)
    s2 = alpha * alpha2
    for n in range(8):
        one, two = s1[:, n : n + 1], s2[:, n : n + 1]
        b, w1, w2 = b_ref[n], w1_ref[n], w2_ref[n]
        solution_ref[n] = one * b - two * w1
        residual_ref[n] = b - one * w1 + two * w2


def shape(*dims):
    return jax.ShapeDtypeStruct(dims, F32)


def call(kernel, name, args, specs, outs, out_specs, scratch=(), flops=0, moved=1 << 20):
    return pl.pallas_call(
        kernel,
        out_shape=outs,
        in_specs=specs,
        out_specs=out_specs,
        scratch_shapes=scratch,
        name=name,
        cost_estimate=pl.CostEstimate(flops=flops, bytes_accessed=moved, transcendentals=0),
    )(*args)


ANY = pl.BlockSpec(memory_space=pl.ANY)
SKIPS = (0, 128, 128, 0)
SPHERE_SCRATCH = [
    pltpu.VMEM((2048, 128), F32),
    pltpu.VMEM((264, 8, 128), F32),
    pltpu.VMEM((2048, 128), F32),
    pltpu.SemaphoreType.DMA(()),
]


def on_device(right_side, potential, orbital_shift, projector, coupling, block_ids):
    plane_high, plane_low, z_band, z_halo, pick = constants()
    bands = (plane_high, plane_low, z_band, z_halo)
    b = right_side.reshape(8, 256, 128)
    pot = potential.reshape(256, 128)
    own = projector.reshape(2048, 128)
    column = lax.axis_index("gz").reshape(1)
    size = lax.axis_size("gz")

    def ring(array, step):
        return lax.ppermute(array, "gz", [(i, (i + step) % 4) for i in range(4)])

    args = (column, block_ids, own, coupling.T, right_side, pick)
    plain, faced, some = shape(ROWS, 128), shape(ROWS + 128, 128), jax.ShapeDtypeStruct((256,), jnp.int32)
    x_edge, y_edge = shape(8, 6, 16, 128), shape(8, 16, 8, 128)
    outs = (plain, faced, plain, faced, some, some, some, some, x_edge, x_edge, y_edge, y_edge)
    scratch = [
        pltpu.SMEM((1024,), jnp.int32),
        pltpu.VMEM((4 * ROWS, 128), F32),
        pltpu.SMEM((4,), jnp.int32),
        pltpu.VMEM((64, 128), F32),
        pltpu.SemaphoreType.DMA((4,)),
        pltpu.SemaphoreType.DMA((4,)),
    ]
    out_specs = (VM,) * 4 + (ANY,) * 8
    here, up, far, down, *lists, x_up, x_down, y_up, y_down = call(
        pack_kernel, "pack", args, [SM] * 2 + [VM] * 4, outs, out_specs, scratch, moved=4 << 20
    )
    lists = (lists[0], ring(lists[1], 1), ring(lists[3], -1), ring(lists[2], 2))
    pieces = (here, ring(up, 1), ring(down, -1), ring(far, 2))
    over = call(over_kernel, "over", lists, [SM] * 4, jax.ShapeDtypeStruct((1,), jnp.int32), SM)

    def whole_column():
        scaled = own.reshape(64, 32, 128) * jnp.sqrt(coupling).reshape(64, 1, 1)
        scaled = scaled.reshape(2048, 128)
        blocks = block_ids.reshape(512)
        ids = jnp.concatenate([blocks, ring(blocks, 1), ring(blocks, -1), ring(blocks, 2)]) - 256 * column[0]
        ids = jnp.where((ids >= 0) & (ids < 256), ids, 256)
        return jnp.concatenate([scaled, ring(scaled, 1), ring(scaled, -1), ring(scaled, 2)]), ids

    def nothing():
        outs = (shape(8192, 128), jax.ShapeDtypeStruct((2048,), jnp.int32))
        return call(nothing_kernel, "nothing", (), [], outs, (ANY, ANY), moved=0)

    everything, ids = lax.cond(over[0] > 0, whole_column, nothing)

    def line(axis, step):
        size = lax.axis_size(axis)
        return [(i, i + step) for i in range(size) if 0 <= i + step < size]

    def halos(x_up, x_down, y_up, y_down):
        return (
            lax.ppermute(x_up, "gx", line("gx", 1)).reshape(8, 96, 128),
            lax.ppermute(x_down, "gx", line("gx", -1)).reshape(8, 96, 128),
            lax.ppermute(y_up, "gy", line("gy", 1)).reshape(8, 128, 128),
            lax.ppermute(y_down, "gy", line("gy", -1)).reshape(8, 128, 128),
        )

    def place(sums, outs, out_specs, *extra):
        args = (*lists, ids, *sums, *pieces, everything, *extra)
        specs = [SM] * 5 + [VM] * 8 + [ANY] + [VM] * len(extra)
        kernel = functools.partial(place_kernel, len(extra) > 1)
        return call(kernel, "place", args, specs, outs, out_specs, SPHERE_SCRATCH, 1 << 32, 7 << 20)

    edges = halos(x_up, x_down, y_up, y_down)
    args = (orbital_shift, column, b, *edges, pieces[1], pieces[2], pot, *bands)
    specs = [SM] * 2 + [VM] * 12
    kernel = functools.partial(stencil_kernel, False, size)
    local = call(kernel, "stencil", args, specs, shape(8, 256, 128), VM, (), 1 << 30, 6 << 20)
    args = (*lists, ids, b.reshape(2048, 128), *pieces, everything)
    specs = [SM] * 5 + [VM] * 5 + [ANY]
    lines_first = [SPHERE_SCRATCH[i] for i in (1, 0, 2, 3)]
    sums = call(project_kernel, "project", args, specs, shape(16, 128), VM, lines_first, 1 << 30, 5 << 20)
    sums = (sums, ring(sums, 1), ring(sums, -1), ring(sums, 2))
    x_edge, y_edge, packed = shape(8, 96, 128), shape(8, 128, 128), shape(144, 128)
    outs = (shape(2048, 128), x_edge, x_edge, y_edge, y_edge, packed, packed, shape(8, 128))
    extra = (local.reshape(2048, 128), b.reshape(2048, 128), pick)
    w1, *edges, up, down, moments = place(sums, outs, (VM,) * 8, *extra)

    opposite, lower, upper = ring(up[:16], 2), ring(up, 1), ring(down, -1)
    edges = halos(*edges)
    w1 = w1.reshape(8, 256, 128)
    args = (orbital_shift, column, w1, *edges, lower, upper, pot, *bands, up, opposite, moments)
    outs = (shape(8, 256, 128), shape(256, 128))
    kernel = functools.partial(stencil_kernel, True, size)
    specs = [SM] * 2 + [VM] * (len(args) - 2)
    local, moments = call(kernel, "stencil", args, specs, outs, (VM,) * 2, (), 1 << 30, 6 << 20)
    moments = lax.all_to_all(moments, GRID, 0, 0, tiled=True)
    w2 = place((up, lower, upper, opposite), shape(2048, 128), VM, local.reshape(2048, 128))
    args = (moments, b, w1, w2.reshape(8, 256, 128))
    outs = (shape(8, 256, 128), shape(8, 256, 128))
    solved, residual = call(finish_kernel, "finish", args, [VM] * 4, outs, (VM,) * 2, (), 0, 5 << 20)
    return solved.reshape(right_side.shape), residual.reshape(right_side.shape)


def solution(mesh):
    field = P(None, *GRID)
    atoms = (P(GRID, None, None, None), P(GRID, None), P(GRID, None))
    return jax.shard_map(
        on_device,
        mesh=mesh,
        in_specs=(field, P(*GRID), P(), *atoms),
        out_specs=(field, field),
        check_vma=False,
    )
```

```python
import functools

import jax
import jax.numpy as jnp
import numpy as np
from jax import lax
from jax.experimental import pallas as pl
from jax.experimental.pallas import tpu as pltpu
from jax.sharding import PartitionSpec as P


STENCIL = (
    -5369.0 / 1800.0,
    12.0 / 7.0,
    -15.0 / 56.0,
    10.0 / 189.0,
    -1.0 / 112.0,
    2.0 / 1925.0,
    -1.0 / 16632.0,
)
GRID = ("gx", "gy", "gz")
F32 = jnp.float32
BF16 = jnp.bfloat16
VM = pl.BlockSpec(memory_space=pltpu.VMEM)
SM = pl.BlockSpec(memory_space=pltpu.SMEM)
NN = (((1,), (0,)), ((), ()))
NT = (((1,), (1,)), ((), ()))
TN = (((0,), (0,)), ((), ()))

OFFSETS = (0, -1, 1, 2)
SLOTS, MOST, BATCH = 200, 188, 12
LIST, FLAG = 32, 20
ROWS = SLOTS * 4


def slot_of(offset):
    return {0: 0, 3: 1, 1: 2, 2: 3}[offset % 4]


def weight(step):
    step = abs(step)
    return -0.5 * STENCIL[step] if 0 < step <= 6 else 0.0


def plane_matrix():
    mat = np.zeros((256, 704))
    for x in range(16):
        for y in range(16):
            row = x * 16 + y
            mat[row, row] = -0.5 * 3.0 * STENCIL[0]
            for reach in range(1, 7):
                for step in (reach, -reach):
                    to_x, to_y = x + step, y + step
                    if 0 <= to_x < 16:
                        mat[row, to_x * 16 + y] += weight(reach)
                    elif to_x < 0:
                        mat[row, 256 + (to_x + 6) * 16 + y] += weight(reach)
                    else:
                        mat[row, 352 + (to_x - 16) * 16 + y] += weight(reach)
                    if 0 <= to_y < 16:
                        mat[row, x * 16 + to_y] += weight(reach)
                    elif to_y < 0:
                        mat[row, 448 + x * 8 + (to_y + 8)] += weight(reach)
                    else:
                        mat[row, 576 + x * 8 + (to_y - 16)] += weight(reach)
    return mat


def z_matrix():
    mat = np.zeros((128, 128))
    for z in range(128):
        for step in range(-6, 7):
            if 0 <= z + step < 128:
                mat[z + step, z] += weight(step)
    return mat


def z_halo_matrix():
    mat = np.zeros((16, 128))
    for z in range(128):
        for reach in range(1, 7):
            if z - reach < 0:
                mat[z - reach + 6, z] += weight(reach)
            if z + reach >= 128:
                mat[8 + z + reach - 128, z] += weight(reach)
    return mat


def pick_matrix():
    mat = np.zeros((16, 128))
    for cell in range(6):
        mat[cell, 122 + cell] = 1.0
        mat[8 + cell, cell] = 1.0
    return mat


def two_parts(mat):
    high = mat.astype(np.float32).astype(BF16)
    low = (mat - high.astype(np.float64)).astype(np.float32).astype(BF16)
    return high, low


def constants():
    plane = two_parts(plane_matrix())
    z_band = np.concatenate(two_parts(z_matrix()))
    z_halo = np.concatenate(two_parts(z_halo_matrix()))
    pick = pick_matrix().astype(np.float32).astype(BF16)
    return tuple(jnp.asarray(part) for part in (*plane, z_band, z_halo, pick))


def dot(lhs, rhs, dims):
    return lax.dot_general(lhs, rhs, dims, preferred_element_type=F32)


def split2(value):
    high = value.astype(BF16)
    return high, (value - high.astype(F32)).astype(BF16)


def split3(value):
    high = value.astype(BF16)
    rest = value - high.astype(F32)
    mid = rest.astype(BF16)
    return high, mid, (rest - mid.astype(F32)).astype(BF16)


def iota(shape, dim):
    return lax.broadcasted_iota(jnp.int32, shape, dim)


def z_faces(value, pick):
    high, mid, low = split3(value)
    return dot(pick, high, NT) + dot(pick, mid, NT) + dot(pick, low, NT)


def pack_kernel(column_ref, ids_ref, own_ref, coupling_ref, v_ref, pick_ref, *rest):
    here_ref, up_ref, opposite_ref, down_ref, *rest = rest
    out_lists, faces_out, (lists_ref, packed, counts, scale_ref, face_done, list_done) = rest[:4], rest[4:8], rest[8:]
    parts = (
        v_ref.at[:, pl.ds(10, 6)],
        v_ref.at[:, pl.ds(0, 6)],
        v_ref.at[:, :, pl.ds(8, 8)],
        v_ref.at[:, :, pl.ds(0, 8)],
    )
    copies = [pltpu.make_async_copy(part, out, face_done.at[i]) for i, (part, out) in enumerate(zip(parts, faces_out))]
    for copy in copies:
        copy.start()
    root = jnp.sqrt(coupling_ref[...])
    for a in range(16):
        scale_ref[a * 4 : a * 4 + 4, :] = jnp.broadcast_to(root[:, a : a + 1], (4, 128))
    for dest in range(4):
        counts[dest] = 0
    packed[...] = jnp.zeros_like(packed)
    column = column_ref[0]

    def atom(a, carry):
        for dest in range(4):
            lists_ref[dest * 256 + a] = counts[dest]
        scale = scale_ref[pl.ds(pl.multiple_of(a * 4, 4), 4), :]
        for k in range(32):
            block = ids_ref[a, k]
            dest = (jnp.right_shift(block, 8) - column) & 3
            taken = counts[dest]
            counts[dest] = taken + 1
            slot = jnp.minimum(taken, SLOTS - 1)
            lists_ref[dest * 256 + LIST + slot] = block & 255
            rows = own_ref[pl.ds(a * 128 + k, 4, stride=32), :] * scale
            packed[pl.ds(pl.multiple_of((dest * SLOTS + slot) * 4, 4), 4), :] = rows
        return carry

    lax.fori_loop(0, 16, atom, 0)
    most = jnp.maximum(jnp.maximum(counts[0], counts[1]), jnp.maximum(counts[2], counts[3]))
    over = (most > MOST).astype(jnp.int32)
    for dest in range(4):
        lists_ref[dest * 256 + 16] = counts[dest]
        lists_ref[dest * 256 + FLAG] = over
    for dest in range(4):
        part = lists_ref.at[pl.ds(dest * 256, 256)]
        copies.append(pltpu.make_async_copy(part, out_lists[dest], list_done.at[dest]))
        copies[-1].start()
    faces = z_faces(v_ref[...].reshape(2048, 128), pick_ref[...])
    for i in range(16):
        up_ref[i * 8 : i * 8 + 8, :] = faces[:8, i * 128 : (i + 1) * 128]
        down_ref[i * 8 : i * 8 + 8, :] = faces[8:, i * 128 : (i + 1) * 128]
    here_ref[...] = packed[:ROWS, :]
    up_ref[128:, :] = packed[ROWS : 2 * ROWS, :]
    opposite_ref[...] = packed[2 * ROWS : 3 * ROWS, :]
    down_ref[128:, :] = packed[3 * ROWS :, :]
    for copy in copies:
        copy.wait()


def over_kernel(lists0, lists1, lists2, lists3, out_ref):
    out_ref[0] = overflow((lists0, lists1, lists2, lists3))


def nothing_kernel(out_ref, ids_ref):
    del out_ref, ids_ref


def z_face(ref, start):
    return jnp.concatenate([ref[start + i * 8 : start + i * 8 + 8, :] for i in range(16)], axis=1)


def sums_at(r, here, lower, upper, opposite):
    rows = []
    for q in range(4):
        total = here[r * 4 + q : r * 4 + q + 1, :]
        for ref, away in ((lower, -1), (upper, 1), (opposite, 2)):
            at = slot_of(OFFSETS[r] - away) * 4 + q
            total = total + ref[at : at + 1, :]
        rows.append(total)
    return jnp.concatenate(rows, axis=1)


def own_form(sums):
    terms = sums * sums
    terms = (terms[:, :128] + terms[:, 128:256]) + (terms[:, 256:384] + terms[:, 384:])
    terms = jnp.broadcast_to(terms, (8, 128))
    for step in (64, 32, 16, 8):
        terms = terms + pltpu.roll(terms, step, axis=1)
    lane = iota((8, 128), 1)
    return jnp.where((lane >= 24) & (lane < 32), terms, 0.0)[0:1]


def stencil_kernel(last, size, shift_ref, column_ref, v_ref, xl, xh, yl, yh, zl, zh, pot, *rest):
    kh_ref, kl_ref, zb_ref, zc_ref, *rest = rest
    if last:
        here, opposite, moment_ref, out_ref, sent_ref = rest
    else:
        (out_ref,) = rest
    start = 16 if last else 0
    below = (column_ref[0] > 0).astype(F32)
    above = (column_ref[0] < size - 1).astype(F32)
    edges = [z_face(zl, start) * below, z_face(zh, start) * above]
    plane_high, plane_low = kh_ref[...], kl_ref[...]
    edge_high, edge_low = split2(jnp.concatenate(edges, axis=0))
    z_halo, z_band = zc_ref[...], zb_ref[...]
    lane, row = iota((8, 128), 1), iota((8, 128), 0)
    moment = jnp.zeros((8, 128), F32)
    for first in range(0, 8, 2):
        pair = (first, first + 1)
        columns = [jnp.concatenate([v_ref[n], xl[n], xh[n], yl[n], yh[n]], axis=0) for n in pair]
        high, low = split2(jnp.concatenate(columns, axis=1))
        plane = dot(plane_high, high, NN) + dot(plane_high, low, NN) + dot(plane_low, high, NN)
        for i, n in enumerate(pair):
            lanes = slice(i * 128, (i + 1) * 128)
            own_high, own_low = high[:256, lanes], low[:256, lanes]
            out = plane[:, lanes] + dot(own_high, z_band[:128], NN)
            out = out + dot(own_low, z_band[:128], NN) + dot(own_high, z_band[128:], NN)
            rows = slice(n * 256, (n + 1) * 256)
            faces_high, faces_low = edge_high[:, rows], edge_low[:, rows]
            out = out + dot(faces_high, z_halo[:16], TN) + dot(faces_low, z_halo[:16], TN)
            out = out + dot(faces_high, z_halo[16:], TN)
            value = v_ref[n]
            out = out + (pot[...] + shift_ref[n]) * value
            if last:
                moment = jnp.where((lane == 3) & (row == n), jnp.sum(value * out), moment)
            out_ref[n] = out
    if last:
        moment = moment + moment_ref[...]
        flat = jnp.zeros((8, 128), F32)
        for i in range(4):
            flat = flat + jnp.where(lane == i * 8 + row, moment[:, i : i + 1], 0.0)
        flat = jnp.sum(flat, axis=0, keepdims=True)
        flat = flat + own_form(sums_at(0, here, zl, zh, opposite))
        sent_ref[...] = jnp.broadcast_to(flat, sent_ref.shape)


def to_lines(src, dst):
    def eight(i, carry):
        for u in range(8):
            line = i * 8 + u
            dst[line] = src[pl.ds(line, 8, stride=256), :]
        return carry

    lax.fori_loop(0, 32, eight, 0)


def overflow(lists):
    return (lists[0][FLAG] | lists[1][FLAG]) | (lists[2][FLAG] | lists[3][FLAG])


def from_all(all_ref, buffer, done, visit):
    def owner(r, carry):
        rows = pl.ds(pl.multiple_of(r * 2048, 2048), 2048)
        copy = pltpu.make_async_copy(all_ref.at[rows, :], buffer, done)
        copy.start()
        copy.wait()
        lax.fori_loop(0, 16, functools.partial(visit, r), 0)
        return carry

    lax.fori_loop(0, 4, owner, 0)


def weight_rows(r, a, j):
    return pl.ds(pl.multiple_of(((r * 16 + a) * 4 + j) * 8, 8), 8)


def batch_of(lists, start, end, size):
    slots = [start + k for k in range(size)]
    return slots, [jnp.where(slot < end, lists[LIST + slot], 256) for slot in slots]


def project_lines(spheres, lines, sums_ref):
    lists, ids_ref, pieces, skips, all_ref, buffer, done = spheres
    over = overflow(lists)

    def add(r, a, sums, slots, at):
        for slot, line in zip(slots, at):
            value = lines[line]
            for j in range(4):
                sums[j] = sums[j] + value * pieces[r][pl.ds(skips[r] + slot * 4 + j, 8, stride=0), :]
        for j in range(4):
            sums_ref[weight_rows(r, a, j), :] = sums[j]

    @pl.when(over == 0)
    def _():
        for r in range(4):

            def atom(a, carry, r=r):
                start, end = lists[r][a], lists[r][a + 1]
                add(r, a, [jnp.zeros((8, 128), F32) for _ in range(4)], *batch_of(lists[r], start, end, BATCH))
                return carry

            def rest(a, carry, r=r):
                start, end = lists[r][a] + BATCH, lists[r][a + 1]

                def four(i, carry):
                    sums = [sums_ref[weight_rows(r, a, j), :] for j in range(4)]
                    add(r, a, sums, *batch_of(lists[r], start + i * 4, end, 4))
                    return carry

                return lax.fori_loop(0, jnp.right_shift(end - start + 3, 2), four, carry)

            lax.fori_loop(0, 16, atom, 0, unroll=2)
            lax.fori_loop(0, 16, rest, 0)

    @pl.when(over != 0)
    def _():
        def visit(r, a, carry):
            sums = [jnp.zeros((8, 128), F32) for _ in range(4)]
            for k in range(32):
                value = lines[ids_ref[(r * 16 + a) * 32 + k]]
                for j in range(4):
                    sums[j] = sums[j] + value * buffer[pl.ds((a * 4 + j) * 32 + k, 8, stride=0), :]
            for j in range(4):
                sums_ref[weight_rows(r, a, j), :] = sums[j]
            return carry

        from_all(all_ref, buffer, done, visit)

    high, mid, low = split3(sums_ref[...])
    ones = jnp.ones((16, 128), BF16)
    return dot(ones, high, NT) + dot(ones, mid, NT) + dot(ones, low, NT)


def place_lines(spheres, lines, weights):
    lists, ids_ref, pieces, skips, all_ref, buffer, done = spheres
    over = overflow(lists)

    def add(of, at, rows):
        values = [lines[line] for line in at]
        for k in range(len(at)):
            terms = [of[j] * rows(k, j) for j in range(4)]
            values[k] = values[k] + ((terms[0] + terms[1]) + (terms[2] + terms[3]))
        for k in range(len(at)):
            lines[at[k]] = values[k]

    @pl.when(over == 0)
    def _():
        for r in range(4):

            def some(a, start, end, size, r=r):
                slots, at = batch_of(lists[r], start, end, size)
                of = [weights[weight_rows(r, a, j), :] for j in range(4)]
                add(of, at, lambda k, j: pieces[r][pl.ds(skips[r] + slots[k] * 4 + j, 8, stride=0), :])

            def atom(a, carry, r=r, some=some):
                some(a, lists[r][a], lists[r][a + 1], BATCH)
                return carry

            def rest(a, carry, r=r, some=some):
                start, end = lists[r][a] + BATCH, lists[r][a + 1]

                def four(i, carry):
                    some(a, start + i * 4, end, 4)
                    return carry

                return lax.fori_loop(0, jnp.right_shift(end - start + 3, 2), four, carry)

            lax.fori_loop(0, 16, atom, 0, unroll=2)
            lax.fori_loop(0, 16, rest, 0)

    @pl.when(over != 0)
    def _():
        def visit(r, a, carry):
            of = [weights[weight_rows(r, a, j), :] for j in range(4)]
            for chunk in range(4):
                at = [ids_ref[(r * 16 + a) * 32 + chunk * 8 + k] for k in range(8)]
                first = chunk * 8
                add(of, at, lambda k, j: buffer[pl.ds((a * 4 + j) * 32 + first + k, 8, stride=0), :])
            return carry

        from_all(all_ref, buffer, done, visit)


def sphere_refs(refs, skips, buffer, done):
    return (refs[:4], refs[4], refs[5:9], skips, refs[9], buffer, done)


def store_rows(total, first, out_refs):
    for row in range(total.shape[1] // 128):
        for ref in out_refs:
            ref[first + row : first + row + 1, :] = total[0:1, row * 128 : (row + 1) * 128]


def project_kernel(lists0, lists1, lists2, lists3, ids_ref, v_ref, *rest):
    pieces, all_ref, out_ref, lines, sums_ref, buffer, done = rest[:4], *rest[4:]
    spheres = sphere_refs((lists0, lists1, lists2, lists3, ids_ref, *pieces, all_ref), SKIPS, buffer, done)
    to_lines(v_ref, lines)
    lines[256] = jnp.zeros((8, 128), F32)
    store_rows(project_lines(spheres, lines, sums_ref), 0, (out_ref,))


def place_kernel(first, lists0, lists1, lists2, lists3, ids_ref, here, lower, upper, opposite, *rest):
    pieces, (all_ref, base_ref) = rest[:4], rest[4:6]
    *rest, weights, lines, buffer, done = rest[6:]
    if first:
        b_ref, pick_ref, out_ref, x_up, x_down, y_up, y_down, up_ref, down_ref, moment_ref = rest
    else:
        (out_ref,) = rest
    spheres = sphere_refs((lists0, lists1, lists2, lists3, ids_ref, *pieces, all_ref), SKIPS, buffer, done)
    rows = [sums_at(r, here, lower, upper, opposite) for r in range(4)]
    high, mid, low = (part.astype(F32) for part in split3(jnp.concatenate(rows, axis=1)))
    row = iota((16, 2048), 0)
    stacked = jnp.where(row == 0, high, jnp.where(row == 1, mid, jnp.where(row == 2, low, 0.0)))
    weights[...] = dot(stacked.astype(BF16), jnp.ones((16, 128), BF16), TN)
    to_lines(base_ref, lines)
    place_lines(spheres, lines, weights)
    if not first:

        def back(i, carry):
            for u in range(8):
                line = i * 8 + u
                out_ref[pl.ds(line, 8, stride=256), :] = lines[line]
            return carry

        lax.fori_loop(0, 32, back, 0)
        return

    def finish(i, moments):
        m0, m1, m2 = moments
        for u in range(8):
            line = i * 8 + u
            image, value = lines[line], b_ref[pl.ds(line, 8, stride=256), :]
            out_ref[pl.ds(line, 8, stride=256), :] = image
            m0, m1, m2 = m0 + value * value, m1 + value * image, m2 + image * image
        return m0, m1, m2

    zero = jnp.zeros((8, 128), F32)
    moments = lax.fori_loop(0, 32, finish, (zero, zero, zero))
    lane = iota((8, 128), 1)
    stored = zero
    for i in range(3):
        stored = jnp.where(lane == i, jnp.sum(moments[i], axis=1, keepdims=True), stored)
    moment_ref[...] = stored
    lines[256] = zero
    total = project_lines(spheres, lines, weights)
    store_rows(total, 0, (up_ref, down_ref))
    image = out_ref[...]
    faces = z_faces(image, pick_ref[...])
    for i in range(16):
        up_ref[16 + i * 8 : 24 + i * 8, :] = faces[:8, i * 128 : (i + 1) * 128]
        down_ref[16 + i * 8 : 24 + i * 8, :] = faces[8:, i * 128 : (i + 1) * 128]
    by_x = image.reshape(8, 256, 128)
    x_up[...] = by_x[:, 160:]
    x_down[...] = by_x[:, :96]
    by_y = image.reshape(128, 2, 8, 128)
    y_up[...] = by_y[:, 1].reshape(8, 128, 128)
    y_down[...] = by_y[:, 0].reshape(8, 128, 128)


def finish_kernel(moments_ref, b_ref, w1_ref, w2_ref, solution_ref, residual_ref):
    flat = jnp.sum(moments_ref[...], axis=0, keepdims=True)
    m0, m1, m2, m3 = (flat[:, i * 8 : (i + 1) * 8] for i in range(4))
    alpha = m0 / m1
    fresh = alpha * (alpha * m2 - 2.0 * m1) + m0
    product = m1 + alpha * (alpha * m3 - 2.0 * m2)
    beta = fresh / m0
    alpha2 = fresh / (product - beta * fresh / alpha)
    s1 = alpha + alpha2 * (1.0 + beta)
    s2 = alpha * alpha2
    for n in range(8):
        one, two = s1[:, n : n + 1], s2[:, n : n + 1]
        b, w1, w2 = b_ref[n], w1_ref[n], w2_ref[n]
        solution_ref[n] = one * b - two * w1
        residual_ref[n] = b - one * w1 + two * w2


def shape(*dims):
    return jax.ShapeDtypeStruct(dims, F32)


def call(kernel, name, args, specs, outs, out_specs, scratch=(), flops=0, moved=1 << 20, room=None):
    return pl.pallas_call(
        kernel,
        out_shape=outs,
        in_specs=specs,
        out_specs=out_specs,
        scratch_shapes=scratch,
        name=name,
        compiler_params=pltpu.CompilerParams(vmem_limit_bytes=room),
        cost_estimate=pl.CostEstimate(flops=flops, bytes_accessed=moved, transcendentals=0),
    )(*args)


ANY = pl.BlockSpec(memory_space=pl.ANY)
ALL_ROWS = 32768
ROOM = 50 << 20
SKIPS = (0, 128, 128, 0)
SPHERE_SCRATCH = [
    pltpu.VMEM((2048, 128), F32),
    pltpu.VMEM((264, 8, 128), F32),
    pltpu.VMEM((2048, 128), F32),
    pltpu.SemaphoreType.DMA(()),
]


def on_device(right_side, potential, orbital_shift, projector, coupling, block_ids):
    plane_high, plane_low, z_band, z_halo, pick = constants()
    bands = (plane_high, plane_low, z_band, z_halo)
    b = right_side.reshape(8, 256, 128)
    pot = potential.reshape(256, 128)
    own = projector.reshape(2048, 128)
    column = lax.axis_index("gz").reshape(1)
    size = lax.axis_size("gz")

    def ring(array, step):
        return lax.ppermute(array, "gz", [(i, (i + step) % 4) for i in range(4)])

    args = (column, block_ids, own, coupling.T, right_side, pick)
    plain, faced, some = shape(ROWS, 128), shape(ROWS + 128, 128), jax.ShapeDtypeStruct((256,), jnp.int32)
    x_edge, y_edge = shape(8, 6, 16, 128), shape(8, 16, 8, 128)
    outs = (plain, faced, plain, faced, some, some, some, some, x_edge, x_edge, y_edge, y_edge)
    scratch = [
        pltpu.SMEM((1024,), jnp.int32),
        pltpu.VMEM((4 * ROWS, 128), F32),
        pltpu.SMEM((4,), jnp.int32),
        pltpu.VMEM((64, 128), F32),
        pltpu.SemaphoreType.DMA((4,)),
        pltpu.SemaphoreType.DMA((4,)),
    ]
    out_specs = (VM,) * 4 + (ANY,) * 8
    here, up, far, down, *lists, x_up, x_down, y_up, y_down = call(
        pack_kernel, "pack", args, [SM] * 2 + [VM] * 4, outs, out_specs, scratch, moved=4 << 20
    )
    lists = (lists[0], ring(lists[1], 1), ring(lists[3], -1), ring(lists[2], 2))
    pieces = (here, ring(up, 1), ring(down, -1), ring(far, 2))
    over = call(over_kernel, "over", lists, [SM] * 4, jax.ShapeDtypeStruct((1,), jnp.int32), SM)

    def whole_column():
        scaled = own.reshape(64, 32, 128) * jnp.sqrt(coupling).reshape(64, 1, 1)
        scaled = scaled.reshape(2048, 128)
        blocks = block_ids.reshape(512)
        ids = jnp.concatenate([blocks, ring(blocks, 1), ring(blocks, -1), ring(blocks, 2)]) - 256 * column[0]
        ids = jnp.where((ids >= 0) & (ids < 256), ids, 256)
        unused = jnp.zeros((ALL_ROWS - 8192, 128), F32)
        return jnp.concatenate([scaled, ring(scaled, 1), ring(scaled, -1), ring(scaled, 2), unused]), ids

    def nothing():
        outs = (shape(ALL_ROWS, 128), jax.ShapeDtypeStruct((2048,), jnp.int32))
        return call(nothing_kernel, "nothing", (), [], outs, (ANY, ANY), moved=0)

    everything, ids = lax.cond(over[0] > 0, whole_column, nothing)

    def line(axis, step):
        size = lax.axis_size(axis)
        return [(i, i + step) for i in range(size) if 0 <= i + step < size]

    def halos(x_up, x_down, y_up, y_down):
        return (
            lax.ppermute(x_up, "gx", line("gx", 1)).reshape(8, 96, 128),
            lax.ppermute(x_down, "gx", line("gx", -1)).reshape(8, 96, 128),
            lax.ppermute(y_up, "gy", line("gy", 1)).reshape(8, 128, 128),
            lax.ppermute(y_down, "gy", line("gy", -1)).reshape(8, 128, 128),
        )

    def place(room, sums, outs, out_specs, *extra):
        args = (*lists, ids, *sums, *pieces, everything, *extra)
        specs = [SM] * 5 + [VM] * 8 + [ANY] + [VM] * len(extra)
        kernel = functools.partial(place_kernel, len(extra) > 1)
        return call(kernel, "place", args, specs, outs, out_specs, SPHERE_SCRATCH, 1 << 32, 7 << 20, room)

    edges = halos(x_up, x_down, y_up, y_down)
    args = (orbital_shift, column, b, *edges, pieces[1], pieces[2], pot, *bands)
    specs = [SM] * 2 + [VM] * 12
    kernel = functools.partial(stencil_kernel, False, size)
    local = call(kernel, "stencil", args, specs, shape(8, 256, 128), VM, (), 1 << 30, 6 << 20, ROOM)
    args = (*lists, ids, b.reshape(2048, 128), *pieces, everything)
    specs = [SM] * 5 + [VM] * 5 + [ANY]
    lines_first = [SPHERE_SCRATCH[i] for i in (1, 0, 2, 3)]
    sums = call(project_kernel, "project", args, specs, shape(16, 128), VM, lines_first, 1 << 30, 5 << 20, ROOM)
    sums = (sums, ring(sums, 1), ring(sums, -1), ring(sums, 2))
    x_edge, y_edge, packed = shape(8, 96, 128), shape(8, 128, 128), shape(144, 128)
    outs = (shape(2048, 128), x_edge, x_edge, y_edge, y_edge, packed, packed, shape(8, 128))
    extra = (local.reshape(2048, 128), b.reshape(2048, 128), pick)
    w1, *edges, up, down, moments = place(ROOM, sums, outs, (VM,) * 8, *extra)

    opposite, lower, upper = ring(up[:16], 2), ring(up, 1), ring(down, -1)
    edges = halos(*edges)
    w1 = w1.reshape(8, 256, 128)
    args = (orbital_shift, column, w1, *edges, lower, upper, pot, *bands, up, opposite, moments)
    outs = (shape(8, 256, 128), shape(256, 128))
    kernel = functools.partial(stencil_kernel, True, size)
    specs = [SM] * 2 + [VM] * (len(args) - 2)
    local, moments = call(kernel, "stencil", args, specs, outs, (VM,) * 2, (), 1 << 30, 6 << 20, ROOM)
    moments = lax.all_to_all(moments, GRID, 0, 0, tiled=True)
    w2 = place(None, (up, lower, upper, opposite), shape(2048, 128), VM, local.reshape(2048, 128))
    args = (moments, b, w1, w2.reshape(8, 256, 128))
    outs = (shape(8, 256, 128), shape(8, 256, 128))
    solved, residual = call(finish_kernel, "finish", args, [VM] * 4, outs, (VM,) * 2, (), 0, 5 << 20)
    return solved.reshape(right_side.shape), residual.reshape(right_side.shape)


def solution(mesh):
    field = P(None, *GRID)
    atoms = (P(GRID, None, None, None), P(GRID, None), P(GRID, None))
    return jax.shard_map(
        on_device,
        mesh=mesh,
        in_specs=(field, P(*GRID), P(), *atoms),
        out_specs=(field, field),
        check_vma=False,
    )
```

```python
import functools

import jax
import jax.numpy as jnp
import numpy as np
from jax import lax
from jax.experimental import pallas as pl
from jax.experimental.pallas import tpu as pltpu
from jax.sharding import PartitionSpec as P


STENCIL = (
    -5369.0 / 1800.0,
    12.0 / 7.0,
    -15.0 / 56.0,
    10.0 / 189.0,
    -1.0 / 112.0,
    2.0 / 1925.0,
    -1.0 / 16632.0,
)
GRID = ("gx", "gy", "gz")
F32 = jnp.float32
BF16 = jnp.bfloat16
VM = pl.BlockSpec(memory_space=pltpu.VMEM)
SM = pl.BlockSpec(memory_space=pltpu.SMEM)
NN = (((1,), (0,)), ((), ()))
NT = (((1,), (1,)), ((), ()))
TN = (((0,), (0,)), ((), ()))

OFFSETS = (0, -1, 1, 2)
SLOTS, MOST, BATCH = 200, 188, 12
LIST, FLAG = 32, 20
ROWS = SLOTS * 4


def slot_of(offset):
    return {0: 0, 3: 1, 1: 2, 2: 3}[offset % 4]


def weight(step):
    step = abs(step)
    return -0.5 * STENCIL[step] if 0 < step <= 6 else 0.0


def plane_matrix():
    mat = np.zeros((256, 704))
    for x in range(16):
        for y in range(16):
            row = x * 16 + y
            mat[row, row] = -0.5 * 3.0 * STENCIL[0]
            for reach in range(1, 7):
                for step in (reach, -reach):
                    to_x, to_y = x + step, y + step
                    if 0 <= to_x < 16:
                        mat[row, to_x * 16 + y] += weight(reach)
                    elif to_x < 0:
                        mat[row, 256 + (to_x + 6) * 16 + y] += weight(reach)
                    else:
                        mat[row, 352 + (to_x - 16) * 16 + y] += weight(reach)
                    if 0 <= to_y < 16:
                        mat[row, x * 16 + to_y] += weight(reach)
                    elif to_y < 0:
                        mat[row, 448 + x * 8 + (to_y + 8)] += weight(reach)
                    else:
                        mat[row, 576 + x * 8 + (to_y - 16)] += weight(reach)
    return mat


def z_matrix():
    mat = np.zeros((128, 128))
    for z in range(128):
        for step in range(-6, 7):
            if 0 <= z + step < 128:
                mat[z + step, z] += weight(step)
    return mat


def z_halo_matrix():
    mat = np.zeros((16, 128))
    for z in range(128):
        for reach in range(1, 7):
            if z - reach < 0:
                mat[z - reach + 6, z] += weight(reach)
            if z + reach >= 128:
                mat[8 + z + reach - 128, z] += weight(reach)
    return mat


def pick_matrix():
    mat = np.zeros((16, 128))
    for cell in range(6):
        mat[cell, 122 + cell] = 1.0
        mat[8 + cell, cell] = 1.0
    return mat


def two_parts(mat):
    high = mat.astype(np.float32).astype(BF16)
    low = (mat - high.astype(np.float64)).astype(np.float32).astype(BF16)
    return high, low


def constants():
    plane = two_parts(plane_matrix())
    z_band = np.concatenate(two_parts(z_matrix()))
    z_halo = np.concatenate(two_parts(z_halo_matrix()))
    pick = pick_matrix().astype(np.float32).astype(BF16)
    return tuple(jnp.asarray(part) for part in (*plane, z_band, z_halo, pick))


def dot(lhs, rhs, dims):
    return lax.dot_general(lhs, rhs, dims, preferred_element_type=F32)


def split2(value):
    high = value.astype(BF16)
    return high, (value - high.astype(F32)).astype(BF16)


def split3(value):
    high = value.astype(BF16)
    rest = value - high.astype(F32)
    mid = rest.astype(BF16)
    return high, mid, (rest - mid.astype(F32)).astype(BF16)


def iota(shape, dim):
    return lax.broadcasted_iota(jnp.int32, shape, dim)


def z_faces(value, pick):
    high, mid, low = split3(value)
    return dot(pick, high, NT) + dot(pick, mid, NT) + dot(pick, low, NT)


def pack_kernel(column_ref, ids_ref, own_ref, coupling_ref, v_ref, pick_ref, *rest):
    here_ref, up_ref, opposite_ref, down_ref, *rest = rest
    out_lists, faces_out, (lists_ref, packed, counts, scale_ref, face_done, list_done) = rest[:4], rest[4:8], rest[8:]
    parts = (
        v_ref.at[:, pl.ds(10, 6)],
        v_ref.at[:, pl.ds(0, 6)],
        v_ref.at[:, :, pl.ds(8, 8)],
        v_ref.at[:, :, pl.ds(0, 8)],
    )
    copies = [pltpu.make_async_copy(part, out, face_done.at[i]) for i, (part, out) in enumerate(zip(parts, faces_out))]
    for copy in copies:
        copy.start()
    root = jnp.sqrt(coupling_ref[...])
    for a in range(16):
        scale_ref[a * 4 : a * 4 + 4, :] = jnp.broadcast_to(root[:, a : a + 1], (4, 128))
    for dest in range(4):
        counts[dest] = 0
    packed[...] = jnp.zeros_like(packed)
    column = column_ref[0]

    def atom(a, carry):
        for dest in range(4):
            lists_ref[dest * 256 + a] = counts[dest]
        scale = scale_ref[pl.ds(pl.multiple_of(a * 4, 4), 4), :]
        for k in range(32):
            block = ids_ref[a, k]
            dest = (jnp.right_shift(block, 8) - column) & 3
            taken = counts[dest]
            counts[dest] = taken + 1
            slot = jnp.minimum(taken, SLOTS - 1)
            lists_ref[dest * 256 + LIST + slot] = block & 255
            rows = own_ref[pl.ds(a * 128 + k, 4, stride=32), :] * scale
            packed[pl.ds(pl.multiple_of((dest * SLOTS + slot) * 4, 4), 4), :] = rows
        return carry

    lax.fori_loop(0, 16, atom, 0)
    most = jnp.maximum(jnp.maximum(counts[0], counts[1]), jnp.maximum(counts[2], counts[3]))
    over = (most > MOST).astype(jnp.int32)
    for dest in range(4):
        lists_ref[dest * 256 + 16] = counts[dest]
        lists_ref[dest * 256 + FLAG] = over
    for dest in range(4):
        part = lists_ref.at[pl.ds(dest * 256, 256)]
        copies.append(pltpu.make_async_copy(part, out_lists[dest], list_done.at[dest]))
        copies[-1].start()
    faces = z_faces(v_ref[...].reshape(2048, 128), pick_ref[...])
    for i in range(16):
        up_ref[i * 8 : i * 8 + 8, :] = faces[:8, i * 128 : (i + 1) * 128]
        down_ref[i * 8 : i * 8 + 8, :] = faces[8:, i * 128 : (i + 1) * 128]
    here_ref[...] = packed[:ROWS, :]
    up_ref[128:, :] = packed[ROWS : 2 * ROWS, :]
    opposite_ref[...] = packed[2 * ROWS : 3 * ROWS, :]
    down_ref[128:, :] = packed[3 * ROWS :, :]
    for copy in copies:
        copy.wait()


def over_kernel(lists0, lists1, lists2, lists3, out_ref):
    out_ref[0] = overflow((lists0, lists1, lists2, lists3))


def nothing_kernel(out_ref, ids_ref):
    del out_ref, ids_ref


def z_face(ref, start):
    return jnp.concatenate([ref[start + i * 8 : start + i * 8 + 8, :] for i in range(16)], axis=1)


def sums_at(r, here, lower, upper, opposite):
    rows = []
    for q in range(4):
        total = here[r * 4 + q : r * 4 + q + 1, :]
        for ref, away in ((lower, -1), (upper, 1), (opposite, 2)):
            at = slot_of(OFFSETS[r] - away) * 4 + q
            total = total + ref[at : at + 1, :]
        rows.append(total)
    return jnp.concatenate(rows, axis=1)


def own_form(sums):
    terms = sums * sums
    terms = (terms[:, :128] + terms[:, 128:256]) + (terms[:, 256:384] + terms[:, 384:])
    terms = jnp.broadcast_to(terms, (8, 128))
    for step in (64, 32, 16, 8):
        terms = terms + pltpu.roll(terms, step, axis=1)
    lane = iota((8, 128), 1)
    return jnp.where((lane >= 24) & (lane < 32), terms, 0.0)[0:1]


def stencil_kernel(last, size, shift_ref, column_ref, v_ref, xl, xh, yl, yh, zl, zh, pot, *rest):
    kh_ref, kl_ref, zb_ref, zc_ref, *rest = rest
    if last:
        here, opposite, moment_ref, out_ref, sent_ref = rest
    else:
        (out_ref,) = rest
    start = 16 if last else 0
    below = (column_ref[0] > 0).astype(F32)
    above = (column_ref[0] < size - 1).astype(F32)
    edges = [z_face(zl, start) * below, z_face(zh, start) * above]
    plane_high, plane_low = kh_ref[...], kl_ref[...]
    edge_high, edge_low = split2(jnp.concatenate(edges, axis=0))
    z_halo, z_band = zc_ref[...], zb_ref[...]
    lane, row = iota((8, 128), 1), iota((8, 128), 0)
    moment = jnp.zeros((8, 128), F32)
    for first in range(0, 8, 2):
        pair = (first, first + 1)
        columns = [jnp.concatenate([v_ref[n], xl[n], xh[n], yl[n], yh[n]], axis=0) for n in pair]
        high, low = split2(jnp.concatenate(columns, axis=1))
        plane = dot(plane_high, high, NN) + dot(plane_high, low, NN) + dot(plane_low, high, NN)
        for i, n in enumerate(pair):
            lanes = slice(i * 128, (i + 1) * 128)
            own_high, own_low = high[:256, lanes], low[:256, lanes]
            out = plane[:, lanes] + dot(own_high, z_band[:128], NN)
            out = out + dot(own_low, z_band[:128], NN) + dot(own_high, z_band[128:], NN)
            rows = slice(n * 256, (n + 1) * 256)
            faces_high, faces_low = edge_high[:, rows], edge_low[:, rows]
            out = out + dot(faces_high, z_halo[:16], TN) + dot(faces_low, z_halo[:16], TN)
            out = out + dot(faces_high, z_halo[16:], TN)
            value = v_ref[n]
            out = out + (pot[...] + shift_ref[n]) * value
            if last:
                moment = jnp.where((lane == 3) & (row == n), jnp.sum(value * out), moment)
            out_ref[n] = out
    if last:
        moment = moment + moment_ref[...]
        flat = jnp.zeros((8, 128), F32)
        for i in range(4):
            flat = flat + jnp.where(lane == i * 8 + row, moment[:, i : i + 1], 0.0)
        flat = jnp.sum(flat, axis=0, keepdims=True)
        flat = flat + own_form(sums_at(0, here, zl, zh, opposite))
        sent_ref[...] = jnp.broadcast_to(flat, sent_ref.shape)


def to_lines(src, dst):
    def eight(i, carry):
        for u in range(8):
            line = i * 8 + u
            dst[line] = src[pl.ds(line, 8, stride=256), :]
        return carry

    lax.fori_loop(0, 32, eight, 0)


def overflow(lists):
    return (lists[0][FLAG] | lists[1][FLAG]) | (lists[2][FLAG] | lists[3][FLAG])


def from_all(all_ref, buffer, done, visit):
    def owner(r, carry):
        rows = pl.ds(pl.multiple_of(r * 2048, 2048), 2048)
        copy = pltpu.make_async_copy(all_ref.at[rows, :], buffer, done)
        copy.start()
        copy.wait()
        lax.fori_loop(0, 16, functools.partial(visit, r), 0)
        return carry

    lax.fori_loop(0, 4, owner, 0)


def weight_rows(r, a, j):
    return pl.ds(pl.multiple_of(((r * 16 + a) * 4 + j) * 8, 8), 8)


def batch_of(lists, start, end, size):
    slots = [start + k for k in range(size)]
    return slots, [jnp.where(slot < end, lists[LIST + slot], 256) for slot in slots]


def project_lines(spheres, lines, sums_ref):
    lists, ids_ref, pieces, skips, all_ref, buffer, done = spheres
    over = overflow(lists)

    def add(r, a, sums, slots, at):
        for slot, line in zip(slots, at):
            value = lines[line]
            for j in range(4):
                sums[j] = sums[j] + value * pieces[r][pl.ds(skips[r] + slot * 4 + j, 8, stride=0), :]
        for j in range(4):
            sums_ref[weight_rows(r, a, j), :] = sums[j]

    @pl.when(over == 0)
    def _():
        for r in range(4):

            def atom(a, carry, r=r):
                start, end = lists[r][a], lists[r][a + 1]
                add(r, a, [jnp.zeros((8, 128), F32) for _ in range(4)], *batch_of(lists[r], start, end, BATCH))
                return carry

            def rest(a, carry, r=r):
                start, end = lists[r][a] + BATCH, lists[r][a + 1]

                def four(i, carry):
                    sums = [sums_ref[weight_rows(r, a, j), :] for j in range(4)]
                    add(r, a, sums, *batch_of(lists[r], start + i * 4, end, 4))
                    return carry

                return lax.fori_loop(0, jnp.right_shift(end - start + 3, 2), four, carry)

            lax.fori_loop(0, 16, atom, 0, unroll=2)
            lax.fori_loop(0, 16, rest, 0)

    @pl.when(over != 0)
    def _():
        def visit(r, a, carry):
            sums = [jnp.zeros((8, 128), F32) for _ in range(4)]
            for k in range(32):
                value = lines[ids_ref[(r * 16 + a) * 32 + k]]
                for j in range(4):
                    sums[j] = sums[j] + value * buffer[pl.ds((a * 4 + j) * 32 + k, 8, stride=0), :]
            for j in range(4):
                sums_ref[weight_rows(r, a, j), :] = sums[j]
            return carry

        from_all(all_ref, buffer, done, visit)

    high, mid, low = split3(sums_ref[...])
    ones = jnp.ones((16, 128), BF16)
    return dot(ones, high, NT) + dot(ones, mid, NT) + dot(ones, low, NT)


def place_lines(spheres, lines, weights):
    lists, ids_ref, pieces, skips, all_ref, buffer, done = spheres
    over = overflow(lists)

    def add(of, at, rows):
        values = [lines[line] for line in at]
        for k in range(len(at)):
            terms = [of[j] * rows(k, j) for j in range(4)]
            values[k] = values[k] + ((terms[0] + terms[1]) + (terms[2] + terms[3]))
        for k in range(len(at)):
            lines[at[k]] = values[k]

    @pl.when(over == 0)
    def _():
        for r in range(4):

            def some(a, start, end, size, r=r):
                slots, at = batch_of(lists[r], start, end, size)
                of = [weights[weight_rows(r, a, j), :] for j in range(4)]
                add(of, at, lambda k, j: pieces[r][pl.ds(skips[r] + slots[k] * 4 + j, 8, stride=0), :])

            def atom(a, carry, r=r, some=some):
                some(a, lists[r][a], lists[r][a + 1], BATCH)
                return carry

            def rest(a, carry, r=r, some=some):
                start, end = lists[r][a] + BATCH, lists[r][a + 1]

                def four(i, carry):
                    some(a, start + i * 4, end, 4)
                    return carry

                return lax.fori_loop(0, jnp.right_shift(end - start + 3, 2), four, carry)

            lax.fori_loop(0, 16, atom, 0, unroll=2)
            lax.fori_loop(0, 16, rest, 0)

    @pl.when(over != 0)
    def _():
        def visit(r, a, carry):
            of = [weights[weight_rows(r, a, j), :] for j in range(4)]
            for chunk in range(4):
                at = [ids_ref[(r * 16 + a) * 32 + chunk * 8 + k] for k in range(8)]
                first = chunk * 8
                add(of, at, lambda k, j: buffer[pl.ds((a * 4 + j) * 32 + first + k, 8, stride=0), :])
            return carry

        from_all(all_ref, buffer, done, visit)


def sphere_refs(refs, skips, buffer, done):
    return (refs[:4], refs[4], refs[5:9], skips, refs[9], buffer, done)


def store_rows(total, first, out_refs):
    for row in range(total.shape[1] // 128):
        for ref in out_refs:
            ref[first + row : first + row + 1, :] = total[0:1, row * 128 : (row + 1) * 128]


def project_kernel(lists0, lists1, lists2, lists3, ids_ref, v_ref, *rest):
    pieces, all_ref, out_ref, lines, sums_ref, buffer, done = rest[:4], *rest[4:]
    spheres = sphere_refs((lists0, lists1, lists2, lists3, ids_ref, *pieces, all_ref), SKIPS, buffer, done)
    to_lines(v_ref, lines)
    lines[256] = jnp.zeros((8, 128), F32)
    store_rows(project_lines(spheres, lines, sums_ref), 0, (out_ref,))


def place_kernel(first, lists0, lists1, lists2, lists3, ids_ref, here, lower, upper, opposite, *rest):
    pieces, (all_ref, base_ref) = rest[:4], rest[4:6]
    *rest, weights, lines, buffer, done = rest[6:]
    if first:
        b_ref, pick_ref, out_ref, x_up, x_down, y_up, y_down, up_ref, down_ref, moment_ref = rest
    else:
        (out_ref,) = rest
    spheres = sphere_refs((lists0, lists1, lists2, lists3, ids_ref, *pieces, all_ref), SKIPS, buffer, done)
    rows = [sums_at(r, here, lower, upper, opposite) for r in range(4)]
    high, mid, low = (part.astype(F32) for part in split3(jnp.concatenate(rows, axis=1)))
    row = iota((16, 2048), 0)
    stacked = jnp.where(row == 0, high, jnp.where(row == 1, mid, jnp.where(row == 2, low, 0.0)))
    weights[...] = dot(stacked.astype(BF16), jnp.ones((16, 128), BF16), TN)
    to_lines(base_ref, lines)
    place_lines(spheres, lines, weights)
    if not first:

        def back(i, carry):
            for u in range(8):
                line = i * 8 + u
                out_ref[pl.ds(line, 8, stride=256), :] = lines[line]
            return carry

        lax.fori_loop(0, 32, back, 0)
        return

    def finish(i, moments):
        m0, m1, m2 = moments
        for u in range(8):
            line = i * 8 + u
            image, value = lines[line], b_ref[pl.ds(line, 8, stride=256), :]
            out_ref[pl.ds(line, 8, stride=256), :] = image
            m0, m1, m2 = m0 + value * value, m1 + value * image, m2 + image * image
        return m0, m1, m2

    zero = jnp.zeros((8, 128), F32)
    moments = lax.fori_loop(0, 32, finish, (zero, zero, zero))
    lane = iota((8, 128), 1)
    stored = zero
    for i in range(3):
        stored = jnp.where(lane == i, jnp.sum(moments[i], axis=1, keepdims=True), stored)
    moment_ref[...] = stored
    lines[256] = zero
    total = project_lines(spheres, lines, weights)
    store_rows(total, 0, (up_ref, down_ref))
    image = out_ref[...]
    faces = z_faces(image, pick_ref[...])
    for i in range(16):
        up_ref[16 + i * 8 : 24 + i * 8, :] = faces[:8, i * 128 : (i + 1) * 128]
        down_ref[16 + i * 8 : 24 + i * 8, :] = faces[8:, i * 128 : (i + 1) * 128]
    by_x = image.reshape(8, 256, 128)
    x_up[...] = by_x[:, 160:]
    x_down[...] = by_x[:, :96]
    by_y = image.reshape(128, 2, 8, 128)
    y_up[...] = by_y[:, 1].reshape(8, 128, 128)
    y_down[...] = by_y[:, 0].reshape(8, 128, 128)


def finish_kernel(moments_ref, b_ref, w1_ref, w2_ref, solution_ref, residual_ref):
    flat = jnp.sum(moments_ref[...], axis=0, keepdims=True)
    m0, m1, m2, m3 = (flat[:, i * 8 : (i + 1) * 8] for i in range(4))
    alpha = m0 / m1
    fresh = alpha * (alpha * m2 - 2.0 * m1) + m0
    product = m1 + alpha * (alpha * m3 - 2.0 * m2)
    beta = fresh / m0
    alpha2 = fresh / (product - beta * fresh / alpha)
    s1 = alpha + alpha2 * (1.0 + beta)
    s2 = alpha * alpha2
    for n in range(8):
        one, two = s1[:, n : n + 1], s2[:, n : n + 1]
        b, w1, w2 = b_ref[n], w1_ref[n], w2_ref[n]
        solution_ref[n] = one * b - two * w1
        residual_ref[n] = b - one * w1 + two * w2


def shape(*dims):
    return jax.ShapeDtypeStruct(dims, F32)


def call(kernel, name, args, specs, outs, out_specs, scratch=(), flops=0, moved=1 << 20, room=None):
    return pl.pallas_call(
        kernel,
        out_shape=outs,
        in_specs=specs,
        out_specs=out_specs,
        scratch_shapes=scratch,
        name=name,
        compiler_params=pltpu.CompilerParams(vmem_limit_bytes=room),
        cost_estimate=pl.CostEstimate(flops=flops, bytes_accessed=moved, transcendentals=0),
    )(*args)


ANY = pl.BlockSpec(memory_space=pl.ANY)
ALL_ROWS = 49152
ROOM = 44 << 20
SKIPS = (0, 128, 128, 0)
SPHERE_SCRATCH = [
    pltpu.VMEM((2048, 128), F32),
    pltpu.VMEM((264, 8, 128), F32),
    pltpu.VMEM((2048, 128), F32),
    pltpu.SemaphoreType.DMA(()),
]


def on_device(right_side, potential, orbital_shift, projector, coupling, block_ids):
    plane_high, plane_low, z_band, z_halo, pick = constants()
    bands = (plane_high, plane_low, z_band, z_halo)
    b = right_side.reshape(8, 256, 128)
    pot = potential.reshape(256, 128)
    own = projector.reshape(2048, 128)
    column = lax.axis_index("gz").reshape(1)
    size = lax.axis_size("gz")

    def ring(array, step):
        return lax.ppermute(array, "gz", [(i, (i + step) % 4) for i in range(4)])

    args = (column, block_ids, own, coupling.T, right_side, pick)
    plain, faced, some = shape(ROWS, 128), shape(ROWS + 128, 128), jax.ShapeDtypeStruct((256,), jnp.int32)
    x_edge, y_edge = shape(8, 6, 16, 128), shape(8, 16, 8, 128)
    outs = (plain, faced, plain, faced, some, some, some, some, x_edge, x_edge, y_edge, y_edge)
    scratch = [
        pltpu.SMEM((1024,), jnp.int32),
        pltpu.VMEM((4 * ROWS, 128), F32),
        pltpu.SMEM((4,), jnp.int32),
        pltpu.VMEM((64, 128), F32),
        pltpu.SemaphoreType.DMA((4,)),
        pltpu.SemaphoreType.DMA((4,)),
    ]
    out_specs = (VM,) * 4 + (ANY,) * 8
    here, up, far, down, *lists, x_up, x_down, y_up, y_down = call(
        pack_kernel, "pack", args, [SM] * 2 + [VM] * 4, outs, out_specs, scratch, moved=4 << 20
    )
    lists = (lists[0], ring(lists[1], 1), ring(lists[3], -1), ring(lists[2], 2))
    pieces = (here, ring(up, 1), ring(down, -1), ring(far, 2))
    over = call(over_kernel, "over", lists, [SM] * 4, jax.ShapeDtypeStruct((1,), jnp.int32), SM)

    def whole_column():
        scaled = own.reshape(64, 32, 128) * jnp.sqrt(coupling).reshape(64, 1, 1)
        scaled = scaled.reshape(2048, 128)
        blocks = block_ids.reshape(512)
        ids = jnp.concatenate([blocks, ring(blocks, 1), ring(blocks, -1), ring(blocks, 2)]) - 256 * column[0]
        ids = jnp.where((ids >= 0) & (ids < 256), ids, 256)
        unused = jnp.zeros((ALL_ROWS - 8192, 128), F32)
        return jnp.concatenate([scaled, ring(scaled, 1), ring(scaled, -1), ring(scaled, 2), unused]), ids

    def nothing():
        outs = (shape(ALL_ROWS, 128), jax.ShapeDtypeStruct((2048,), jnp.int32))
        return call(nothing_kernel, "nothing", (), [], outs, (ANY, ANY), moved=0)

    everything, ids = lax.cond(over[0] > 0, whole_column, nothing)

    def line(axis, step):
        size = lax.axis_size(axis)
        return [(i, i + step) for i in range(size) if 0 <= i + step < size]

    def halos(x_up, x_down, y_up, y_down):
        return (
            lax.ppermute(x_up, "gx", line("gx", 1)).reshape(8, 96, 128),
            lax.ppermute(x_down, "gx", line("gx", -1)).reshape(8, 96, 128),
            lax.ppermute(y_up, "gy", line("gy", 1)).reshape(8, 128, 128),
            lax.ppermute(y_down, "gy", line("gy", -1)).reshape(8, 128, 128),
        )

    def place(room, sums, outs, out_specs, *extra):
        args = (*lists, ids, *sums, *pieces, everything, *extra)
        specs = [SM] * 5 + [VM] * 8 + [ANY] + [VM] * len(extra)
        kernel = functools.partial(place_kernel, len(extra) > 1)
        return call(kernel, "place", args, specs, outs, out_specs, SPHERE_SCRATCH, 1 << 32, 7 << 20, room)

    edges = halos(x_up, x_down, y_up, y_down)
    args = (orbital_shift, column, b, *edges, pieces[1], pieces[2], pot, *bands)
    specs = [SM] * 2 + [VM] * 12
    kernel = functools.partial(stencil_kernel, False, size)
    local = call(kernel, "stencil", args, specs, shape(8, 256, 128), VM, (), 1 << 30, 6 << 20, ROOM)
    args = (*lists, ids, b.reshape(2048, 128), *pieces, everything)
    specs = [SM] * 5 + [VM] * 5 + [ANY]
    lines_first = [SPHERE_SCRATCH[i] for i in (1, 0, 2, 3)]
    sums = call(project_kernel, "project", args, specs, shape(16, 128), VM, lines_first, 1 << 30, 5 << 20, ROOM)
    sums = (sums, ring(sums, 1), ring(sums, -1), ring(sums, 2))
    x_edge, y_edge, packed = shape(8, 96, 128), shape(8, 128, 128), shape(144, 128)
    outs = (shape(2048, 128), x_edge, x_edge, y_edge, y_edge, packed, packed, shape(8, 128))
    extra = (local.reshape(2048, 128), b.reshape(2048, 128), pick)
    w1, *edges, up, down, moments = place(ROOM, sums, outs, (VM,) * 8, *extra)

    opposite, lower, upper = ring(up[:16], 2), ring(up, 1), ring(down, -1)
    edges = halos(*edges)
    w1 = w1.reshape(8, 256, 128)
    args = (orbital_shift, column, w1, *edges, lower, upper, pot, *bands, up, opposite, moments)
    outs = (shape(8, 256, 128), shape(256, 128))
    kernel = functools.partial(stencil_kernel, True, size)
    specs = [SM] * 2 + [VM] * (len(args) - 2)
    local, moments = call(kernel, "stencil", args, specs, outs, (VM,) * 2, (), 1 << 30, 6 << 20, ROOM)
    moments = lax.all_to_all(moments, GRID, 0, 0, tiled=True)
    w2 = place(None, (up, lower, upper, opposite), shape(2048, 128), VM, local.reshape(2048, 128))
    args = (moments, b, w1, w2.reshape(8, 256, 128))
    outs = (shape(8, 256, 128), shape(8, 256, 128))
    solved, residual = call(finish_kernel, "finish", args, [VM] * 4, outs, (VM,) * 2, (), 0, 5 << 20)
    return solved.reshape(right_side.shape), residual.reshape(right_side.shape)


def solution(mesh):
    field = P(None, *GRID)
    atoms = (P(GRID, None, None, None), P(GRID, None), P(GRID, None))
    return jax.shard_map(
        on_device,
        mesh=mesh,
        in_specs=(field, P(*GRID), P(), *atoms),
        out_specs=(field, field),
        check_vma=False,
    )
```
